32 devices in a mesh: groups: 2 (over y), seq: 4 (over z), tensor: 4 (over x, core).
Axes of the slice: x: 2, y: 2, z: 4, core: 2. Of those that a mesh axis runs over, the one named last changes fastest.
Arguments:
- video_query: bfloat16 [1024, 4096], P(('groups', 'seq'), 'tensor'), parts along dimension 0, may hold values from -21 to 21
- video_key: bfloat16 [1024, 4096], P(('groups', 'seq'), 'tensor'), parts along dimension 0, may hold values from -21 to 21
- video_value: bfloat16 [1024, 4096], P(('groups', 'seq'), 'tensor'), parts along dimension 0, may hold values from -6 to 6
- video_stream: bfloat16 [1024, 4096], P(('groups', 'seq'), 'tensor'), parts along dimension 0, may hold values from -6 to 6
- out_weight: bfloat16 [4096, 4096], P('tensor'), may hold values from -0.09375 to 0.09375
- cross_query: bfloat16 [1024, 2048], P(('groups', 'seq'), 'tensor'), parts along dimension 0, may hold values from -21 to 21
- audio_key: bfloat16 [128, 2048], P(('groups', 'seq'), 'tensor'), parts along dimension 0, may hold values from -21 to 21
- audio_value: bfloat16 [128, 2048], P(('groups', 'seq'), 'tensor'), parts along dimension 0, may hold values from -6 to 6
- audio_query: bfloat16 [128, 2048], P(('groups', 'seq'), 'tensor'), parts along dimension 0, may hold values from -21 to 21
- cross_key: bfloat16 [1024, 2048], P(('groups', 'seq'), 'tensor'), parts along dimension 0, may hold values from -21 to 21
- cross_value: bfloat16 [1024, 2048], P(('groups', 'seq'), 'tensor'), parts along dimension 0, may hold values from -6 to 6
Outputs:
- video_next: bfloat16 [1024, 4096], P(('groups', 'seq'), 'tensor'), parts along dimension 0
- video_cross: bfloat16 [1024, 2048], P(('groups', 'seq'), 'tensor'), parts along dimension 0
- audio_cross: bfloat16 [128, 2048], P(('groups', 'seq'), 'tensor'), parts along dimension 0
The draws below stay inside these ranges and needn't reach their ends.
There are 2 independent parts, one for each index of `groups`. The reference program is written for one: setup_inputs(seed, part) draws one part's arguments, and reference() takes and returns one part's arrays. A program takes and returns all parts, laid end to end along the dimension named above; an argument that names none is the same for every part. Nothing has to cross between parts.
All inputs are finite; a program needn't handle non-finite values.
Results may differ from the reference program's by a relative error of at most 0.012.
Values may be sent and summed in bfloat16 or wider, within the bound.
A program may use at most 64 MiB of HBM per device.

```python
import math
import jax
import jax.numpy as jnp
from jax import lax

DV = 4096
DA = 2048
HV = 32
HA = 16
HD = 128
VT = 512
AT = 64


def paired(key, query_rows, key_rows, width, salt):
    subkeys = jax.random.split(jax.random.fold_in(key, salt), 2)
    queries = jnp.clip(1.5 * jax.random.normal(subkeys[0], (query_rows, width), jnp.float32), -6.0, 6.0)
    keyset = jnp.clip(1.5 * jax.random.normal(subkeys[1], (key_rows, width), jnp.float32), -6.0, 6.0)
    return (queries, keyset)


def draw_video_query(key, part):
    return paired(key, VT, VT, DV, 11)[0].astype(jnp.bfloat16)


def draw_video_key(key, part):
    return paired(key, VT, VT, DV, 11)[1].astype(jnp.bfloat16)


def draw_cross_query(key, part):
    return paired(key, VT, AT, DA, 23)[0].astype(jnp.bfloat16)


def draw_audio_key(key, part):
    return paired(key, VT, AT, DA, 23)[1].astype(jnp.bfloat16)


def draw_audio_query(key, part):
    return paired(key, AT, VT, DA, 37)[0].astype(jnp.bfloat16)


def draw_cross_key(key, part):
    return paired(key, AT, VT, DA, 37)[1].astype(jnp.bfloat16)


def block_levels(stream_key, shape, pieces, low, largest):
    def one(position, shards_of):
        heights = jax.random.uniform(jax.random.fold_in(jax.random.fold_in(stream_key, 6), position), (shards_of,), jnp.float32, low / len(pieces), largest / len(pieces))
        return jnp.repeat(jnp.exp(heights), shape[position] // shards_of).reshape((-1,) + (1,) * (len(shape) - position - 1))

    factor_of = one(*pieces[0])
    for cut in pieces[1:]:
        factor_of = factor_of * one(*cut)
    return factor_of


def bell_draw(key, dims, spread, limit, pieces=(), held_as=jnp.bfloat16):
    entries = spread * jax.random.normal(key, dims, jnp.float32)
    if pieces:
        entries = entries * block_levels(key, dims, pieces, -0.22, 0.18)
    return jnp.clip(entries, -limit, limit).astype(held_as)


def setup_inputs(seed: int = 0, part: int = 0) -> dict:
    arg_keys = jax.random.split(jax.random.key(seed), 12)
    part_keys = jax.random.split(jax.random.fold_in(arg_keys[11], part), 12)
    return {
        "video_query": draw_video_query(jax.random.fold_in(jax.random.fold_in(arg_keys[11], part), 71), part),
        "video_key": draw_video_key(jax.random.fold_in(jax.random.fold_in(arg_keys[11], part), 71), part),
        "video_value": bell_draw(part_keys[2], (VT, DV), 1.0, 6.0, ((0, 4), (1, 4))),
        "video_stream": bell_draw(part_keys[3], (VT, DV), 1.0, 6.0, ((0, 4), (1, 4))),
        "out_weight": bell_draw(arg_keys[4], (DV, DV), DV ** -0.5, 0.09375, ((0, 4),)),
        "cross_query": draw_cross_query(jax.random.fold_in(jax.random.fold_in(arg_keys[11], part), 71), part),
        "audio_key": draw_audio_key(jax.random.fold_in(jax.random.fold_in(arg_keys[11], part), 71), part),
        "audio_value": bell_draw(part_keys[7], (AT, DA), 1.0, 6.0, ((0, 4), (1, 4))),
        "audio_query": draw_audio_query(jax.random.fold_in(jax.random.fold_in(arg_keys[11], part), 71), part),
        "cross_key": draw_cross_key(jax.random.fold_in(jax.random.fold_in(arg_keys[11], part), 71), part),
        "cross_value": bell_draw(part_keys[10], (VT, DA), 1.0, 6.0, ((0, 4), (1, 4))),
    }


def attend(queries, keyset, values, head_count):
    query_rows = queries.shape[0]
    key_rows = keyset.shape[0]
    query_head = queries.reshape(query_rows, head_count, HD).transpose(1, 0, 2)
    key_head = keyset.reshape(key_rows, head_count, HD).transpose(1, 0, 2)
    value_head = values.reshape(key_rows, head_count, HD).transpose(1, 0, 2)

    def single(operands):
        query_one, key_one, value_one = operands
        scores = jnp.dot(query_one, key_one.T, preferred_element_type=jnp.float32) * (1.0 / math.sqrt(HD))
        row_max = lax.optimization_barrier(jnp.max(scores, axis=1, keepdims=True))
        raised = jnp.exp(scores - row_max)
        row_sum = lax.optimization_barrier(jnp.sum(raised, axis=1, keepdims=True))
        weights = raised.astype(jnp.bfloat16)
        return jnp.dot(weights, value_one, preferred_element_type=jnp.float32) / row_sum
    result = lax.map(single, (query_head, key_head, value_head))
    return result.transpose(1, 0, 2).reshape(query_rows, head_count * HD)

def reference(video_query, video_key, video_value, video_stream, out_weight, cross_query, audio_key, audio_value, audio_query, cross_key, cross_value):
    video_heads = attend(video_query, video_key, video_value, HV).astype(jnp.bfloat16)
    projected = jnp.dot(video_heads, out_weight, preferred_element_type=jnp.float32)
    video_next = (video_stream.astype(jnp.float32) + projected).astype(jnp.bfloat16)
    video_cross = attend(cross_query, audio_key, audio_value, HA).astype(jnp.bfloat16)
    audio_cross = attend(audio_query, cross_key, cross_value, HA).astype(jnp.bfloat16)
    return (video_next, video_cross, audio_cross)
```

```python
import functools
import math

import jax
import jax.numpy as jnp
from jax import lax
from jax.experimental import pallas as pl
from jax.experimental.pallas import tpu as pltpu
from jax.sharding import PartitionSpec as P

HD = 128


def blank_state(query_rows, head_count):
    return (
        jnp.full((head_count, query_rows), -1e30, jnp.float32),
        jnp.zeros((head_count, query_rows), jnp.float32),
        jnp.zeros((head_count, query_rows, HD), jnp.float32),
    )


def absorb(carried, queries, keyset, values, head_count):
    running, row_sum, numerator = carried
    query_rows = queries.shape[0]
    key_rows = keyset.shape[0]
    factor = 1.0 / math.sqrt(HD)
    query_heads = queries.reshape(query_rows, head_count, HD)
    for offset in range(0, key_rows, 1024):
        width_keys = min(1024, key_rows - offset)
        key_block = keyset[offset : offset + width_keys].reshape(width_keys, head_count, HD)
        value_block = values[offset : offset + width_keys].reshape(width_keys, head_count, HD)
        scores = (
            jnp.einsum("qhd,khd->hqk", query_heads, key_block, preferred_element_type=jnp.float32)
            * factor
        )
        highest = jnp.maximum(running, jnp.max(scores, axis=2))
        raised = jnp.exp(scores - highest[:, :, None])
        shrink = jnp.exp(running - highest)
        row_sum = row_sum * shrink + jnp.sum(raised, axis=2)
        numerator = numerator * shrink[:, :, None] + jnp.einsum(
            "hqk,khd->hqd",
            raised.astype(jnp.bfloat16),
            value_block,
            preferred_element_type=jnp.float32,
        )
        running = highest
    return (running, row_sum, numerator)


def finish(carried, head_count):
    running, row_sum, numerator = carried
    result = numerator / row_sum[:, :, None]
    return result.transpose(1, 0, 2).reshape(result.shape[1], head_count * HD).astype(jnp.bfloat16)


def local(
    video_query,
    video_key,
    video_value,
    video_stream,
    out_weight,
    cross_query,
    audio_key,
    audio_value,
    audio_query,
    cross_key,
    cross_value,
):
    local_heads = video_query.shape[1] // HD
    query_rows = video_query.shape[0]
    pieces = (
        lax.all_gather(video_key, "seq", axis=0, tiled=True),
        lax.all_gather(video_value, "seq", axis=0, tiled=True),
    )
    carried_video = absorb(
        blank_state(query_rows, local_heads), video_query, pieces[0], pieces[1], local_heads
    )
    attended = finish(carried_video, local_heads)
    projected = jnp.dot(attended, out_weight, preferred_element_type=jnp.float32)
    summed = lax.psum_scatter(
        projected.astype(jnp.bfloat16), "tensor", scatter_dimension=1, tiled=True
    ).astype(jnp.float32)
    video_next = (video_stream.astype(jnp.float32) + summed).astype(jnp.bfloat16)
    cross_heads = cross_query.shape[1] // HD
    every_key, every_value = (
        lax.all_gather(audio_key, "seq", axis=0, tiled=True),
        lax.all_gather(audio_value, "seq", axis=0, tiled=True),
    )
    carried_audio = absorb(
        blank_state(cross_query.shape[0], cross_heads),
        cross_query,
        every_key,
        every_value,
        cross_heads,
    )
    video_cross = finish(carried_audio, cross_heads)
    pieces = (
        lax.all_gather(cross_key, "seq", axis=0, tiled=True),
        lax.all_gather(cross_value, "seq", axis=0, tiled=True),
    )
    carried_cross = absorb(
        blank_state(audio_query.shape[0], cross_heads),
        audio_query,
        pieces[0],
        pieces[1],
        cross_heads,
    )
    audio_cross = finish(carried_cross, cross_heads)
    return (video_next, video_cross, audio_cross)


MESH = pl.DeviceIdType.MESH
NT = (((1,), (1,)), ((), ()))
WIDE = 512
SHARES = (3, 3, 2)


def softmax_parts(queries, keyset, values):
    scores = lax.dot_general(queries, keyset, NT, preferred_element_type=jnp.float32) * (
        1.0 / math.sqrt(HD)
    )
    highest = jnp.max(scores, axis=1, keepdims=True)
    raised = jnp.exp(scores - highest)
    row_sum = jnp.sum(raised, axis=1, keepdims=True)
    numerator = jnp.dot(raised.astype(jnp.bfloat16), values, preferred_element_type=jnp.float32)
    return highest, row_sum, numerator


def row_cuts(rows):
    tiles, whole = rows // 16, sum(SHARES)
    marks = sorted({tiles * sum(SHARES[: i + 1]) // whole for i in range(len(SHARES))} | {0})
    return [(16 * a, 16 * (b - a)) for a, b in zip(marks, marks[1:])]


def by_distance(me, seq):
    right = (me < seq - 1 - me).astype(jnp.int32)
    toward = 2 * right - 1
    short = right * me + (1 - right) * (seq - 1 - me)
    order = []
    for i in range(seq - 1):
        both = (i < 2 * short).astype(jnp.int32)
        near = (i // 2 + 1) * (1 if i % 2 == 0 else -1)
        order.append(me + toward * (both * near + (1 - both) * (i - short + 1)))
    return order


def block_kernel(
    seq,
    tensor,
    vq,
    vk,
    vv,
    vs,
    weight,
    cq,
    ak,
    av,
    aq,
    ck,
    cv,
    next_ref,
    vcross_ref,
    across_ref,
    kv,
    q_all,
    heads_out,
    gathered,
    audio,
    partial,
    stats,
    partial_in,
    stats_in,
    cross_v,
    stream_v,
    weight_v,
    kept,
    mine,
    pair_out,
    pair_in,
    far_out,
    far_in,
    token,
    kv_send,
    kv_recv,
    q_send,
    q_recv,
    own_kv,
    own_q,
    out_send,
    out_recv,
    audio_send,
    audio_recv,
    audio_own,
    part_send,
    part_recv,
    stat_send,
    stat_recv,
    cross_sem,
    stream_sem,
    weight_sem,
    pair_send,
    pair_recv,
    home_recv,
    far_send,
    far_recv,
):
    rows = vq.shape[0]
    span = vq.shape[1] // seq
    share = span // HD
    cross_heads = cq.shape[1] // HD
    audio_rows = aq.shape[0]
    chips = tensor // 2
    width = next_ref.shape[1]
    pieces = width // WIDE
    cuts = row_cuts(rows)
    groups = len(cuts)
    me = lax.axis_index("seq")
    place = lax.axis_index("tensor")
    core = lax.rem(place, 2)
    chip = place // 2
    sibling = chip * 2 + (1 - core)
    peers = by_distance(me, seq)
    far_chips = [lax.rem(chip + d, chips) for d in range(chips)]

    def rows_of(p):
        return pl.ds(pl.multiple_of(p * rows, rows), rows)

    def audio_rows_of(p):
        return pl.ds(pl.multiple_of(p * audio_rows, audio_rows), audio_rows)

    def cols_of(p):
        return pl.ds(pl.multiple_of(p * span, span), span)

    def slot(p, r):
        start, size = cuts[r]
        return pl.ds(pl.multiple_of(seq * start + p * size, 16), size)

    for kind, ref in enumerate((vk, vv)):
        pltpu.make_async_copy(ref.at[:, cols_of(me)], kv.at[kind, rows_of(me)], own_kv).start()
    for r in range(groups):
        pltpu.make_async_copy(vq.at[pl.ds(*cuts[r]), cols_of(me)], q_all.at[slot(me, r)], own_q).start()
    for kind, ref in enumerate((ak, av, aq)):
        pltpu.make_async_copy(ref, audio.at[kind, audio_rows_of(me)], audio_own).start()
    for kind, ref in enumerate((cq, ck, cv)):
        pltpu.make_async_copy(ref, cross_v.at[kind], cross_sem).start()
    stream_copy = pltpu.make_async_copy(vs, stream_v, stream_sem)
    stream_copy.start()

    def local_done(ref, sem):
        pltpu.make_async_copy(ref, ref, sem).wait()

    barrier = pltpu.get_barrier_semaphore()
    for way in (1, -1):

        @pl.when((me + way >= 0) & (me + way < seq))
        def _():
            pl.semaphore_signal(barrier, inc=1, device_id={"seq": me + way}, device_id_type=MESH)

    pl.semaphore_signal(barrier, inc=1, device_id={"tensor": sibling}, device_id_type=MESH)
    for d in range(1, chips):
        pl.semaphore_signal(
            barrier, inc=1, device_id={"tensor": far_chips[d] * 2 + core}, device_id_type=MESH
        )
    inner = ((me > 0) & (me < seq - 1)).astype(jnp.int32)
    with jax.named_scope("barrier"):
        pl.semaphore_wait(barrier, chips + 1 + inner)

    def to_seq(src, dst, send_sem, recv_sem, p):
        return pltpu.make_async_remote_copy(
            src_ref=src,
            dst_ref=dst,
            send_sem=send_sem,
            recv_sem=recv_sem,
            device_id={"seq": p},
            device_id_type=MESH,
        )

    def all_of(ref, send_sem, recv_sem):
        return to_seq(ref, ref, send_sem, recv_sem, peers[0])

    def keys_to(p):
        for kind, ref in enumerate((vk, vv)):
            to_seq(ref.at[:, cols_of(p)], kv.at[kind, rows_of(me)], kv_send, kv_recv, p).start()

    def send_queries(r):
        here = pl.ds(*cuts[r])
        for p in peers:
            to_seq(vq.at[here, cols_of(p)], q_all.at[slot(me, r)], q_send, q_recv.at[r], p).start()

    def audio_hop(step, way):
        shard = lax.rem(me - way * step + seq, seq)
        here = audio_rows_of(shard)
        return to_seq(
            audio.at[:, here],
            audio.at[:, here],
            audio_send.at[(way + 1) // 2],
            audio_recv.at[shard],
            lax.rem(me + way + seq, seq),
        )

    def on_line(step, way):
        source, target = me - way * step, me + way
        return (source >= 0) & (source < seq) & (target >= 0) & (target < seq)

    def pass_audio(step):
        for way in (1, -1):

            @pl.when(on_line(step, way))
            def _():
                copy = audio_hop(step, way)
                if step:
                    copy.wait_recv()
                    audio_hop(step - 1, way).wait_send()
                copy.start()

    def end_audio():
        for step in range(1, seq):
            for way in (1, -1):
                source, target = me - way * step, me + way
                last = (target < 0) | (target >= seq)

                @pl.when((source >= 0) & (source < seq) & last)
                def _():
                    audio_hop(step, way).wait_recv()

    def pass_token(way):
        index = (way + 1) // 2

        @pl.when((me - 2 * way >= 0) & (me - 2 * way < seq))
        def _():
            pl.semaphore_wait(token.at[index], 1)

        @pl.when(
            (me - way >= 0) & (me - way < seq) & (me + way >= 0) & (me + way < seq)
        )
        def _():
            pl.semaphore_signal(
                token.at[index], inc=1, device_id={"seq": me + way}, device_id_type=MESH
            )

    local_done(audio.at[:, audio_rows_of(0)], audio_own)
    pass_audio(0)
    keys_to(peers[0])
    with jax.named_scope("tokens"):
        pass_token(1)
        pass_token(-1)
    for p in peers[1:]:
        keys_to(p)
    with jax.named_scope("pass1"):
        pass_audio(1)
    for r in range(groups):
        send_queries(r)
    weight_copy = pltpu.make_async_copy(weight, weight_v, weight_sem)
    weight_copy.start()

    def wait_keys():
        local_done(kv.at[:, rows_of(0)], own_kv)
        local_done(q_all.at[rows_of(0)], own_q)
        all_of(kv.at[:, pl.ds(0, (seq - 1) * rows)], kv_send, kv_recv).wait_recv()

    def attend_rows(r):
        start, size = cuts[r]
        all_of(q_all.at[pl.ds(0, (seq - 1) * size)], q_send, q_recv.at[r]).wait_recv()
        block = pl.ds(seq * start, seq * size)
        for h in range(share):
            cols = slice(h * HD, (h + 1) * HD)
            _, row_sum, numerator = softmax_parts(q_all[block, cols], kv[0, :, cols], kv[1, :, cols])
            heads_out[block, cols] = (numerator / row_sum).astype(jnp.bfloat16)
        here = pl.ds(start, size)
        for p in peers:
            to_seq(heads_out.at[slot(p, r)], gathered.at[me, here], out_send, out_recv.at[r], p).start()
        gathered[me, here] = heads_out[slot(me, r)]

    def cross_audio():
        local_done(cross_v, cross_sem)
        end_audio()
        lane = lax.broadcasted_iota(jnp.int32, (seq * audio_rows, HD), 1)
        held = jnp.zeros((seq * audio_rows, HD), jnp.float32)
        for c in range(cross_heads):
            cols = slice(c * HD, (c + 1) * HD)
            highest, row_sum, numerator = softmax_parts(
                audio[2, :, cols], cross_v[1, :, cols], cross_v[2, :, cols]
            )
            held = jnp.where(lane == c, highest, held)
            held = jnp.where(lane == cross_heads + c, row_sum, held)
            partial[:, cols] = numerator.astype(jnp.bfloat16)
        stats[...] = held

    def cross_video():
        for c in range(cross_heads):
            cols = slice(c * HD, (c + 1) * HD)
            _, row_sum, numerator = softmax_parts(
                cross_v[0, :, cols], audio[0, :, cols], audio[1, :, cols]
            )
            vcross_ref[:, cols] = (numerator / row_sum).astype(jnp.bfloat16)

    def cross_send():
        for p in peers:
            theirs = audio_rows_of(p)
            to_seq(partial.at[theirs], partial_in.at[me], part_send, part_recv, p).start()
            to_seq(stats.at[theirs], stats_in.at[me], stat_send, stat_recv, p).start()

    def cross_finish():
        all_of(partial_in.at[pl.ds(0, seq - 1)], part_send, part_recv).wait_recv()
        all_of(stats_in.at[pl.ds(0, seq - 1)], stat_send, stat_recv).wait_recv()
        my_audio = audio_rows_of(me)
        held = [stats[my_audio, :]] + [stats_in[p] for p in peers]
        for c in range(cross_heads):
            cols = slice(c * HD, (c + 1) * HD)
            parts = [partial[my_audio, cols]] + [partial_in[p, :, cols] for p in peers]
            tops = [s[:, c : c + 1] for s in held]
            sums = [s[:, cross_heads + c : cross_heads + c + 1] for s in held]
            highest = functools.reduce(jnp.maximum, tops)
            factors = [jnp.exp(t - highest) for t in tops]
            row_sum = sum(f * s for f, s in zip(factors, sums))
            numerator = sum(f * n.astype(jnp.float32) for f, n in zip(factors, parts))
            across_ref[:, cols] = (numerator / row_sum).astype(jnp.bfloat16)

    def product(attended, d, side, j):
        target = far_chips[d] * 2 + (core if side else 1 - core)
        cols = pl.ds(pl.multiple_of(target * width + j * WIDE, WIDE), WIDE)
        return jnp.dot(attended, weight_v[:, cols], preferred_element_type=jnp.float32)

    def pair_copy(r, d):
        here = pl.ds(*cuts[r])
        return pltpu.make_async_remote_copy(
            src_ref=pair_out.at[d, here],
            dst_ref=pair_in.at[d, here],
            send_sem=pair_send,
            recv_sem=pair_recv.at[r, d - 1],
            device_id={"tensor": sibling},
            device_id_type=MESH,
        )

    def far_copy(r, d):
        here = pl.ds(*cuts[r])
        return pltpu.make_async_remote_copy(
            src_ref=far_out.at[d - 1, here],
            dst_ref=far_in.at[d - 1, here],
            send_sem=far_send,
            recv_sem=far_recv.at[r, d - 1],
            device_id={"tensor": far_chips[d] * 2 + core},
            device_id_type=MESH,
        )

    home_copy = pltpu.make_async_remote_copy(
        src_ref=pair_out.at[0],
        dst_ref=pair_in.at[0],
        send_sem=pair_send,
        recv_sem=home_recv,
        device_id={"tensor": sibling},
        device_id_type=MESH,
    )
    blocks = [slice(j * WIDE, (j + 1) * WIDE) for j in range(pieces)]

    def share_rows(r):
        here = pl.ds(*cuts[r])
        all_of(gathered.at[pl.ds(0, seq - 1), here], out_send, out_recv.at[r]).wait_recv()
        attended = jnp.concatenate([gathered[p, here] for p in range(seq)], axis=1)
        if r == 0:
            weight_copy.wait()
        for d in range(1, chips):
            for j, block in enumerate(blocks):
                pair_out[d, here, block] = product(attended, d, 0, j).astype(jnp.bfloat16)
            pair_copy(r, d).start()
        for d in range(1, chips):
            for j, block in enumerate(blocks):
                mine[d - 1, here, block] = product(attended, d, 1, j)
        for d in range(1, chips):
            pair_copy(r, d).wait_recv()
            far_out[d - 1, here] = (mine[d - 1, here] + pair_in[d, here].astype(jnp.float32)).astype(
                jnp.bfloat16
            )
            far_copy(r, d).start()

    def keep_rows():
        attended = jnp.concatenate([gathered[p] for p in range(seq)], axis=1)
        for j, block in enumerate(blocks):
            pair_out[0, :, block] = product(attended, 0, 0, j).astype(jnp.bfloat16)
        home_copy.start()
        stream_copy.wait()
        for j, block in enumerate(blocks):
            kept[:, block] = product(attended, 0, 1, j) + stream_v[:, block].astype(jnp.float32)

    def close_rows(r):
        here = pl.ds(*cuts[r])
        value = kept[here] + pair_in[0, here].astype(jnp.float32)
        for d in range(1, chips):
            far_copy(r, d).wait_recv()
            value = value + far_in[d - 1, here].astype(jnp.float32)
        next_ref[here] = value.astype(jnp.bfloat16)

    def settle():
        all_of(kv.at[:, pl.ds(0, (seq - 1) * rows)], kv_send, kv_recv).wait_send()
        all_of(q_all.at[pl.ds(0, (seq - 1) * rows)], q_send, q_recv.at[0]).wait_send()
        all_of(heads_out.at[pl.ds(0, (seq - 1) * rows)], out_send, out_recv.at[0]).wait_send()
        all_of(partial.at[pl.ds(0, (seq - 1) * audio_rows)], part_send, part_recv).wait_send()
        all_of(stats.at[pl.ds(0, (seq - 1) * audio_rows)], stat_send, stat_recv).wait_send()
        for way in (1, -1):
            for step in range(seq - 1):

                @pl.when(on_line(step, way) & jnp.logical_not(on_line(step + 1, way)))
                def _():
                    audio_hop(step, way).wait_send()

        all_of(pair_out, pair_send, pair_recv.at[0, 0]).wait_send()
        if chips > 1:
            all_of(far_out, far_send, far_recv.at[0, 0]).wait_send()

    with jax.named_scope("wait_keys"):
        wait_keys()
    for r in range(groups):
        with jax.named_scope(f"attend{r}"):
            attend_rows(r)
        if r == 0:
            with jax.named_scope("pass2"):
                for step in range(2, seq - 1):
                    pass_audio(step)
    with jax.named_scope("cross_audio"):
        cross_audio()
    with jax.named_scope("cross_video"):
        cross_video()
    for r in range(groups):
        if r == groups - 1:
            with jax.named_scope("cross_send"):
                cross_send()
        with jax.named_scope(f"share{r}"):
            share_rows(r)
    with jax.named_scope("keep"):
        keep_rows()
    with jax.named_scope("cross_finish"):
        cross_finish()
    with jax.named_scope("wait_home"):
        home_copy.wait_recv()
    for r in range(groups):
        with jax.named_scope(f"close{r}"):
            close_rows(r)
    with jax.named_scope("settle"):
        settle()


def write_out(*refs):
    half = len(refs) // 2
    for src, dst in zip(refs[:half], refs[half:]):
        dst[...] = src[...]


def fused(seq, tensor, *operands):
    vq, vk, vv, vs, weight, cq, ak, av, aq, ck, cv = operands
    rows, features = vq.shape
    span = features // seq
    audio_rows, cross_width = aq.shape
    chips = tensor // 2
    width = weight.shape[1] // tensor
    groups = len(row_cuts(rows))
    others = max(chips - 1, 1)
    bf16, f32, dma = jnp.bfloat16, jnp.float32, pltpu.SemaphoreType.DMA
    shapes = tuple(jax.ShapeDtypeStruct(x.shape, bf16) for x in (vs, cq, aq))
    whole = pl.BlockSpec(memory_space=pltpu.VMEM)
    results = pl.pallas_call(
        functools.partial(block_kernel, seq, tensor),
        out_shape=tuple(pltpu.VMEM(x.shape, bf16) for x in (vs, cq, aq)),
        in_specs=[pl.BlockSpec(memory_space=pltpu.HBM)] * 11,
        out_specs=(whole,) * 3,
        scratch_shapes=[
            pltpu.VMEM((2, seq * rows, span), bf16),
            pltpu.VMEM((seq * rows, span), bf16),
            pltpu.VMEM((seq * rows, span), bf16),
            pltpu.VMEM((seq, rows, span), bf16),
            pltpu.VMEM((3, seq * audio_rows, cross_width), bf16),
            pltpu.VMEM((seq * audio_rows, cross_width), bf16),
            pltpu.VMEM((seq * audio_rows, HD), f32),
            pltpu.VMEM((seq, audio_rows, cross_width), bf16),
            pltpu.VMEM((seq, audio_rows, HD), f32),
            pltpu.VMEM((3, *cq.shape), bf16),
            pltpu.VMEM(vs.shape, bf16),
            pltpu.VMEM(weight.shape, bf16),
            pltpu.VMEM(vs.shape, f32),
            pltpu.VMEM((others, rows, width), f32),
            pltpu.VMEM((chips, rows, width), bf16),
            pltpu.VMEM((chips, rows, width), bf16),
            pltpu.VMEM((others, rows, width), bf16),
            pltpu.VMEM((others, rows, width), bf16),
            pltpu.SemaphoreType.REGULAR((2,)),
            dma(()),
            dma(()),
            dma(()),
            dma((groups,)),
            dma(()),
            dma(()),
            dma(()),
            dma((groups,)),
            dma((2,)),
            dma((seq,)),
            dma(()),
            dma(()),
            dma(()),
            dma(()),
            dma(()),
            dma(()),
            dma(()),
            dma(()),
            dma(()),
            dma((groups, others)),
            dma(()),
            dma(()),
            dma((groups, others)),
        ],
        compiler_params=pltpu.CompilerParams(
            collective_id=0, has_side_effects=True, vmem_limit_bytes=60000000
        ),
    )(*operands)
    return pl.pallas_call(
        write_out,
        out_shape=shapes,
        in_specs=[whole] * 3,
        out_specs=(whole,) * 3,
        compiler_params=pltpu.CompilerParams(vmem_limit_bytes=8 * 2**20),
    )(*results)


def fits(mesh, operands):
    seq, tensor = mesh.shape["seq"], mesh.shape["tensor"]
    vq, weight, cq, aq = operands[0], operands[4], operands[5], operands[8]
    return (
        seq > 1
        and (vq.shape[1] // HD) % seq == 0
        and tensor % 2 == 0
        and (weight.shape[1] // tensor) % WIDE == 0
        and aq.shape[0] % 16 == 0
        and vq.shape[0] % 16 == 0
        and 2 * (cq.shape[1] // HD) <= HD
        and weight.size * 2 <= 10 * 2**20
        and vq.shape[0] <= 128
        and seq <= 8
    )


def solution(mesh):
    def step(*operands):
        if fits(mesh, operands):
            return fused(mesh.shape["seq"], mesh.shape["tensor"], *operands)
        return local(*operands)

    in_specs = (
        P(("groups", "seq"), "tensor"),
        P(("groups", "seq"), "tensor"),
        P(("groups", "seq"), "tensor"),
        P(("groups", "seq"), "tensor"),
        P("tensor", None),
        P(("groups", "seq"), "tensor"),
        P(("groups", "seq"), "tensor"),
        P(("groups", "seq"), "tensor"),
        P(("groups", "seq"), "tensor"),
        P(("groups", "seq"), "tensor"),
        P(("groups", "seq"), "tensor"),
    )
    out_specs = (
        P(("groups", "seq"), "tensor"),
        P(("groups", "seq"), "tensor"),
        P(("groups", "seq"), "tensor"),
    )
    return jax.shard_map(step, mesh=mesh, in_specs=in_specs, out_specs=out_specs, check_vma=False)
```

```python
import functools
import math

import jax
import jax.numpy as jnp
from jax import lax
from jax.experimental import pallas as pl
from jax.experimental.pallas import tpu as pltpu
from jax.sharding import PartitionSpec as P

HD = 128


def blank_state(query_rows, head_count):
    return (
        jnp.full((head_count, query_rows), -1e30, jnp.float32),
        jnp.zeros((head_count, query_rows), jnp.float32),
        jnp.zeros((head_count, query_rows, HD), jnp.float32),
    )


def absorb(carried, queries, keyset, values, head_count):
    running, row_sum, numerator = carried
    query_rows = queries.shape[0]
    key_rows = keyset.shape[0]
    factor = 1.0 / math.sqrt(HD)
    query_heads = queries.reshape(query_rows, head_count, HD)
    for offset in range(0, key_rows, 1024):
        width_keys = min(1024, key_rows - offset)
        key_block = keyset[offset : offset + width_keys].reshape(width_keys, head_count, HD)
        value_block = values[offset : offset + width_keys].reshape(width_keys, head_count, HD)
        scores = (
            jnp.einsum("qhd,khd->hqk", query_heads, key_block, preferred_element_type=jnp.float32)
            * factor
        )
        highest = jnp.maximum(running, jnp.max(scores, axis=2))
        raised = jnp.exp(scores - highest[:, :, None])
        shrink = jnp.exp(running - highest)
        row_sum = row_sum * shrink + jnp.sum(raised, axis=2)
        numerator = numerator * shrink[:, :, None] + jnp.einsum(
            "hqk,khd->hqd",
            raised.astype(jnp.bfloat16),
            value_block,
            preferred_element_type=jnp.float32,
        )
        running = highest
    return (running, row_sum, numerator)


def finish(carried, head_count):
    running, row_sum, numerator = carried
    result = numerator / row_sum[:, :, None]
    return result.transpose(1, 0, 2).reshape(result.shape[1], head_count * HD).astype(jnp.bfloat16)


def local(
    video_query,
    video_key,
    video_value,
    video_stream,
    out_weight,
    cross_query,
    audio_key,
    audio_value,
    audio_query,
    cross_key,
    cross_value,
):
    local_heads = video_query.shape[1] // HD
    query_rows = video_query.shape[0]
    pieces = (
        lax.all_gather(video_key, "seq", axis=0, tiled=True),
        lax.all_gather(video_value, "seq", axis=0, tiled=True),
    )
    carried_video = absorb(
        blank_state(query_rows, local_heads), video_query, pieces[0], pieces[1], local_heads
    )
    attended = finish(carried_video, local_heads)
    projected = jnp.dot(attended, out_weight, preferred_element_type=jnp.float32)
    summed = lax.psum_scatter(
        projected.astype(jnp.bfloat16), "tensor", scatter_dimension=1, tiled=True
    ).astype(jnp.float32)
    video_next = (video_stream.astype(jnp.float32) + summed).astype(jnp.bfloat16)
    cross_heads = cross_query.shape[1] // HD
    every_key, every_value = (
        lax.all_gather(audio_key, "seq", axis=0, tiled=True),
        lax.all_gather(audio_value, "seq", axis=0, tiled=True),
    )
    carried_audio = absorb(
        blank_state(cross_query.shape[0], cross_heads),
        cross_query,
        every_key,
        every_value,
        cross_heads,
    )
    video_cross = finish(carried_audio, cross_heads)
    pieces = (
        lax.all_gather(cross_key, "seq", axis=0, tiled=True),
        lax.all_gather(cross_value, "seq", axis=0, tiled=True),
    )
    carried_cross = absorb(
        blank_state(audio_query.shape[0], cross_heads),
        audio_query,
        pieces[0],
        pieces[1],
        cross_heads,
    )
    audio_cross = finish(carried_cross, cross_heads)
    return (video_next, video_cross, audio_cross)


MESH = pl.DeviceIdType.MESH
NT = (((1,), (1,)), ((), ()))
WIDE = 512
SHARES = (3, 3, 2)


def softmax_parts(queries, keyset, values):
    scores = lax.dot_general(queries, keyset, NT, preferred_element_type=jnp.float32) * (
        1.0 / math.sqrt(HD)
    )
    highest = jnp.max(scores, axis=1, keepdims=True)
    raised = jnp.exp(scores - highest)
    row_sum = jnp.sum(raised, axis=1, keepdims=True)
    numerator = jnp.dot(raised.astype(jnp.bfloat16), values, preferred_element_type=jnp.float32)
    return highest, row_sum, numerator


def row_cuts(rows):
    tiles, whole = rows // 16, sum(SHARES)
    marks = sorted({tiles * sum(SHARES[: i + 1]) // whole for i in range(len(SHARES))} | {0})
    return [(16 * a, 16 * (b - a)) for a, b in zip(marks, marks[1:])]


def by_distance(me, seq):
    right = (me < seq - 1 - me).astype(jnp.int32)
    toward = 2 * right - 1
    short = right * me + (1 - right) * (seq - 1 - me)
    order = []
    for i in range(seq - 1):
        both = (i < 2 * short).astype(jnp.int32)
        near = (i // 2 + 1) * (1 if i % 2 == 0 else -1)
        order.append(me + toward * (both * near + (1 - both) * (i - short + 1)))
    return order


def block_kernel(
    seq,
    tensor,
    vq,
    vk,
    vv,
    vs,
    weight,
    cq,
    ak,
    av,
    aq,
    ck,
    cv,
    next_ref,
    vcross_ref,
    across_ref,
    kv,
    q_all,
    heads_out,
    gathered,
    audio,
    partial,
    stats,
    partial_in,
    stats_in,
    cross_v,
    stream_v,
    weight_v,
    kept,
    mine,
    pair_out,
    pair_in,
    far_out,
    far_in,
    token,
    beside,
    kv_send,
    kv_recv,
    q_send,
    q_recv,
    own_kv,
    own_q,
    out_send,
    out_recv,
    audio_send,
    audio_recv,
    audio_own,
    part_send,
    part_recv,
    stat_send,
    stat_recv,
    cross_sem,
    stream_sem,
    weight_sem,
    pair_send,
    pair_recv,
    home_recv,
    far_send,
    far_recv,
):
    rows = vq.shape[0]
    span = vq.shape[1] // seq
    share = span // HD
    cross_heads = cq.shape[1] // HD
    audio_rows = aq.shape[0]
    chips = tensor // 2
    width = next_ref.shape[1]
    pieces = width // WIDE
    cuts = row_cuts(rows)
    groups = len(cuts)
    me = lax.axis_index("seq")
    place = lax.axis_index("tensor")
    core = lax.rem(place, 2)
    chip = place // 2
    sibling = chip * 2 + (1 - core)
    peers = by_distance(me, seq)
    far_chips = [lax.rem(chip + d, chips) for d in range(chips)]

    def rows_of(p):
        return pl.ds(pl.multiple_of(p * rows, rows), rows)

    def audio_rows_of(p):
        return pl.ds(pl.multiple_of(p * audio_rows, audio_rows), audio_rows)

    def cols_of(p):
        return pl.ds(pl.multiple_of(p * span, span), span)

    def slot(p, r):
        start, size = cuts[r]
        return pl.ds(pl.multiple_of(seq * start + p * size, 16), size)

    for kind, ref in enumerate((vk, vv)):
        pltpu.make_async_copy(ref.at[:, cols_of(me)], kv.at[kind, rows_of(me)], own_kv).start()
    for r in range(groups):
        pltpu.make_async_copy(vq.at[pl.ds(*cuts[r]), cols_of(me)], q_all.at[slot(me, r)], own_q).start()
    for kind, ref in enumerate((ak, av, aq)):
        pltpu.make_async_copy(ref, audio.at[kind, audio_rows_of(me)], audio_own).start()
    for kind, ref in enumerate((cq, ck, cv)):
        pltpu.make_async_copy(ref, cross_v.at[kind], cross_sem).start()
    stream_copy = pltpu.make_async_copy(vs, stream_v, stream_sem)
    stream_copy.start()

    def local_done(ref, sem):
        pltpu.make_async_copy(ref, ref, sem).wait()

    barrier = pltpu.get_barrier_semaphore()
    for way in (1, -1):

        @pl.when((me + way >= 0) & (me + way < seq))
        def _():
            pl.semaphore_signal(barrier, inc=1, device_id={"seq": me + way}, device_id_type=MESH)

    pl.semaphore_signal(barrier, inc=1, device_id={"tensor": sibling}, device_id_type=MESH)
    for d in range(1, chips):
        pl.semaphore_signal(
            barrier, inc=1, device_id={"tensor": far_chips[d] * 2 + core}, device_id_type=MESH
        )
    inner = ((me > 0) & (me < seq - 1)).astype(jnp.int32)
    with jax.named_scope("barrier"):
        pl.semaphore_wait(barrier, chips + 1 + inner)

    def to_seq(src, dst, send_sem, recv_sem, p):
        return pltpu.make_async_remote_copy(
            src_ref=src,
            dst_ref=dst,
            send_sem=send_sem,
            recv_sem=recv_sem,
            device_id={"seq": p},
            device_id_type=MESH,
        )

    def all_of(ref, send_sem, recv_sem):
        return to_seq(ref, ref, send_sem, recv_sem, peers[0])

    def keys_to(p, kinds=(0, 1)):
        for kind, ref in zip(kinds, (vk, vv)[kinds[0] :]):
            to_seq(ref.at[:, cols_of(p)], kv.at[kind, rows_of(me)], kv_send, kv_recv, p).start()

    def send_queries(r):
        here = pl.ds(*cuts[r])
        for p in peers[::-1]:
            to_seq(vq.at[here, cols_of(p)], q_all.at[slot(me, r)], q_send, q_recv.at[r], p).start()

    def audio_hop(step, way):
        shard = lax.rem(me - way * step + seq, seq)
        here = audio_rows_of(shard)
        return to_seq(
            audio.at[:, here],
            audio.at[:, here],
            audio_send.at[(way + 1) // 2],
            audio_recv.at[shard],
            lax.rem(me + way + seq, seq),
        )

    def on_line(step, way):
        source, target = me - way * step, me + way
        return (source >= 0) & (source < seq) & (target >= 0) & (target < seq)

    def pass_audio(step):
        for way in (1, -1):

            @pl.when(on_line(step, way))
            def _():
                copy = audio_hop(step, way)
                if step:
                    copy.wait_recv()
                    audio_hop(step - 1, way).wait_send()
                copy.start()

    def end_audio():
        for step in range(1, seq):
            for way in (1, -1):
                source, target = me - way * step, me + way
                last = (target < 0) | (target >= seq)

                @pl.when((source >= 0) & (source < seq) & last)
                def _():
                    audio_hop(step, way).wait_recv()

    def pass_token(way):
        index = (way + 1) // 2

        @pl.when((me - 2 * way >= 0) & (me - 2 * way < seq))
        def _():
            pl.semaphore_wait(token.at[index], 1)

        @pl.when(
            (me - way >= 0) & (me - way < seq) & (me + way >= 0) & (me + way < seq)
        )
        def _():
            pl.semaphore_signal(
                token.at[index], inc=1, device_id={"seq": me + way}, device_id_type=MESH
            )

    local_done(audio.at[:, audio_rows_of(0)], audio_own)
    def run(name, f, *args):
        with jax.named_scope(name):
            f(*args)

    def tokens():
        pass_token(1)
        pass_token(-1)

    def late_audio():
        for step in range(2, seq - 1):
            pass_audio(step)

    def meet():
        pl.semaphore_signal(
            beside.at[0], inc=1, device_id={"tensor": sibling}, device_id_type=MESH
        )
        pl.semaphore_wait(beside.at[0], 1)

    run("p0", pass_audio, 0)
    run("K0", keys_to, peers[0])
    run("tok", tokens)
    run("sib", meet)
    run("K1", keys_to, peers[1])
    run("K2", keys_to, peers[2])
    run("p1", pass_audio, 1)
    run("q0", send_queries, 0)
    weight_copy = pltpu.make_async_copy(weight, weight_v, weight_sem)
    weight_copy.start()

    def wait_keys():
        local_done(kv.at[:, rows_of(0)], own_kv)
        local_done(q_all.at[rows_of(0)], own_q)
        all_of(kv.at[:, pl.ds(0, (seq - 1) * rows)], kv_send, kv_recv).wait_recv()

    def attend_rows(r):
        start, size = cuts[r]
        all_of(q_all.at[pl.ds(0, (seq - 1) * size)], q_send, q_recv.at[r]).wait_recv()
        block = pl.ds(seq * start, seq * size)
        for h in range(share):
            cols = slice(h * HD, (h + 1) * HD)
            _, row_sum, numerator = softmax_parts(q_all[block, cols], kv[0, :, cols], kv[1, :, cols])
            heads_out[block, cols] = (numerator / row_sum).astype(jnp.bfloat16)
        here = pl.ds(start, size)
        for p in peers[::-1]:
            to_seq(heads_out.at[slot(p, r)], gathered.at[me, here], out_send, out_recv.at[r], p).start()
        gathered[me, here] = heads_out[slot(me, r)]

    def cross_audio():
        local_done(cross_v, cross_sem)
        end_audio()
        lane = lax.broadcasted_iota(jnp.int32, (seq * audio_rows, HD), 1)
        held = jnp.zeros((seq * audio_rows, HD), jnp.float32)
        for c in range(cross_heads):
            cols = slice(c * HD, (c + 1) * HD)
            highest, row_sum, numerator = softmax_parts(
                audio[2, :, cols], cross_v[1, :, cols], cross_v[2, :, cols]
            )
            held = jnp.where(lane == c, highest, held)
            held = jnp.where(lane == cross_heads + c, row_sum, held)
            partial[:, cols] = numerator.astype(jnp.bfloat16)
        stats[...] = held

    def cross_video():
        for c in range(cross_heads):
            cols = slice(c * HD, (c + 1) * HD)
            _, row_sum, numerator = softmax_parts(
                cross_v[0, :, cols], audio[0, :, cols], audio[1, :, cols]
            )
            vcross_ref[:, cols] = (numerator / row_sum).astype(jnp.bfloat16)

    def cross_send():
        for p in peers:
            theirs = audio_rows_of(p)
            to_seq(partial.at[theirs], partial_in.at[me], part_send, part_recv, p).start()
            to_seq(stats.at[theirs], stats_in.at[me], stat_send, stat_recv, p).start()

    def cross_finish():
        all_of(partial_in.at[pl.ds(0, seq - 1)], part_send, part_recv).wait_recv()
        all_of(stats_in.at[pl.ds(0, seq - 1)], stat_send, stat_recv).wait_recv()
        my_audio = audio_rows_of(me)
        held = [stats[my_audio, :]] + [stats_in[p] for p in peers]
        for c in range(cross_heads):
            cols = slice(c * HD, (c + 1) * HD)
            parts = [partial[my_audio, cols]] + [partial_in[p, :, cols] for p in peers]
            tops = [s[:, c : c + 1] for s in held]
            sums = [s[:, cross_heads + c : cross_heads + c + 1] for s in held]
            highest = functools.reduce(jnp.maximum, tops)
            factors = [jnp.exp(t - highest) for t in tops]
            row_sum = sum(f * s for f, s in zip(factors, sums))
            numerator = sum(f * n.astype(jnp.float32) for f, n in zip(factors, parts))
            across_ref[:, cols] = (numerator / row_sum).astype(jnp.bfloat16)

    def product(attended, d, side, j):
        target = far_chips[d] * 2 + (core if side else 1 - core)
        cols = pl.ds(pl.multiple_of(target * width + j * WIDE, WIDE), WIDE)
        return jnp.dot(attended, weight_v[:, cols], preferred_element_type=jnp.float32)

    def pair_copy(r, d):
        here = pl.ds(*cuts[r])
        return pltpu.make_async_remote_copy(
            src_ref=pair_out.at[d, here],
            dst_ref=pair_in.at[d, here],
            send_sem=pair_send,
            recv_sem=pair_recv.at[r, d - 1],
            device_id={"tensor": sibling},
            device_id_type=MESH,
        )

    def far_copy(r, d):
        here = pl.ds(*cuts[r])
        return pltpu.make_async_remote_copy(
            src_ref=far_out.at[d - 1, here],
            dst_ref=far_in.at[d - 1, here],
            send_sem=far_send,
            recv_sem=far_recv.at[r, d - 1],
            device_id={"tensor": far_chips[d] * 2 + core},
            device_id_type=MESH,
        )

    home_copy = pltpu.make_async_remote_copy(
        src_ref=pair_out.at[0],
        dst_ref=pair_in.at[0],
        send_sem=pair_send,
        recv_sem=home_recv,
        device_id={"tensor": sibling},
        device_id_type=MESH,
    )
    blocks = [slice(j * WIDE, (j + 1) * WIDE) for j in range(pieces)]

    def share_rows(r):
        here = pl.ds(*cuts[r])
        all_of(gathered.at[pl.ds(0, seq - 1), here], out_send, out_recv.at[r]).wait_recv()
        attended = jnp.concatenate([gathered[p, here] for p in range(seq)], axis=1)
        if r == 0:
            weight_copy.wait()
        for d in range(1, chips):
            for j, block in enumerate(blocks):
                pair_out[d, here, block] = product(attended, d, 0, j).astype(jnp.bfloat16)
            pair_copy(r, d).start()
        for d in range(1, chips):
            for j, block in enumerate(blocks):
                mine[d - 1, here, block] = product(attended, d, 1, j)

    def send_far(r):
        here = pl.ds(*cuts[r])
        for d in range(1, chips):
            pair_copy(r, d).wait_recv()
            far_out[d - 1, here] = (mine[d - 1, here] + pair_in[d, here].astype(jnp.float32)).astype(
                jnp.bfloat16
            )
            far_copy(r, d).start()

    def all_heads():
        return jnp.concatenate([gathered[p] for p in range(seq)], axis=1)

    def give_home():
        attended = all_heads()
        for j, block in enumerate(blocks):
            pair_out[0, :, block] = product(attended, 0, 0, j).astype(jnp.bfloat16)
        home_copy.start()

    def keep_home():
        attended = all_heads()
        stream_copy.wait()
        for j, block in enumerate(blocks):
            kept[:, block] = product(attended, 0, 1, j) + stream_v[:, block].astype(jnp.float32)

    def close_rows(r):
        here = pl.ds(*cuts[r])
        value = kept[here] + pair_in[0, here].astype(jnp.float32)
        for d in range(1, chips):
            far_copy(r, d).wait_recv()
            value = value + far_in[d - 1, here].astype(jnp.float32)
        next_ref[here] = value.astype(jnp.bfloat16)

    def settle():
        all_of(kv.at[:, pl.ds(0, (seq - 1) * rows)], kv_send, kv_recv).wait_send()
        all_of(q_all.at[pl.ds(0, (seq - 1) * rows)], q_send, q_recv.at[0]).wait_send()
        all_of(heads_out.at[pl.ds(0, (seq - 1) * rows)], out_send, out_recv.at[0]).wait_send()
        all_of(partial.at[pl.ds(0, (seq - 1) * audio_rows)], part_send, part_recv).wait_send()
        all_of(stats.at[pl.ds(0, (seq - 1) * audio_rows)], stat_send, stat_recv).wait_send()
        for way in (1, -1):
            for step in range(seq - 1):

                @pl.when(on_line(step, way) & jnp.logical_not(on_line(step + 1, way)))
                def _():
                    audio_hop(step, way).wait_send()

        all_of(pair_out, pair_send, pair_recv.at[0, 0]).wait_send()
        if chips > 1:
            all_of(far_out, far_send, far_recv.at[0, 0]).wait_send()

    run("wk", wait_keys)
    run("q1", send_queries, 1)
    run("p2", late_audio)
    run("a0", attend_rows, 0)
    run("q2", send_queries, 2)
    run("a1", attend_rows, 1)
    run("ca", cross_audio)
    run("A0", share_rows, 0)
    run("a2", attend_rows, 2)
    run("B0", send_far, 0)
    run("A1", share_rows, 1)
    run("B1", send_far, 1)
    run("cs", cross_send)
    run("A2", share_rows, 2)
    run("k0", give_home)
    run("B2", send_far, 2)
    run("cv", cross_video)
    run("k1", keep_home)
    run("cf", cross_finish)
    run("h", home_copy.wait_recv)
    run("c0", close_rows, 0)
    run("c1", close_rows, 1)
    run("c2", close_rows, 2)
    with jax.named_scope("settle"):
        settle()


def write_out(*refs):
    half = len(refs) // 2
    for src, dst in zip(refs[:half], refs[half:]):
        dst[...] = src[...]


def fused(seq, tensor, *operands):
    vq, vk, vv, vs, weight, cq, ak, av, aq, ck, cv = operands
    rows, features = vq.shape
    span = features // seq
    audio_rows, cross_width = aq.shape
    chips = tensor // 2
    width = weight.shape[1] // tensor
    groups = len(row_cuts(rows))
    others = max(chips - 1, 1)
    bf16, f32, dma = jnp.bfloat16, jnp.float32, pltpu.SemaphoreType.DMA
    shapes = tuple(jax.ShapeDtypeStruct(x.shape, bf16) for x in (vs, cq, aq))
    whole = pl.BlockSpec(memory_space=pltpu.VMEM)
    results = pl.pallas_call(
        functools.partial(block_kernel, seq, tensor),
        out_shape=tuple(pltpu.VMEM(x.shape, bf16) for x in (vs, cq, aq)),
        in_specs=[pl.BlockSpec(memory_space=pltpu.HBM)] * 11,
        out_specs=(whole,) * 3,
        scratch_shapes=[
            pltpu.VMEM((2, seq * rows, span), bf16),
            pltpu.VMEM((seq * rows, span), bf16),
            pltpu.VMEM((seq * rows, span), bf16),
            pltpu.VMEM((seq, rows, span), bf16),
            pltpu.VMEM((3, seq * audio_rows, cross_width), bf16),
            pltpu.VMEM((seq * audio_rows, cross_width), bf16),
            pltpu.VMEM((seq * audio_rows, HD), f32),
            pltpu.VMEM((seq, audio_rows, cross_width), bf16),
            pltpu.VMEM((seq, audio_rows, HD), f32),
            pltpu.VMEM((3, *cq.shape), bf16),
            pltpu.VMEM(vs.shape, bf16),
            pltpu.VMEM(weight.shape, bf16),
            pltpu.VMEM(vs.shape, f32),
            pltpu.VMEM((others, rows, width), f32),
            pltpu.VMEM((chips, rows, width), bf16),
            pltpu.VMEM((chips, rows, width), bf16),
            pltpu.VMEM((others, rows, width), bf16),
            pltpu.VMEM((others, rows, width), bf16),
            pltpu.SemaphoreType.REGULAR((2,)),
            pltpu.SemaphoreType.REGULAR((1,)),
            dma(()),
            dma(()),
            dma(()),
            dma((groups,)),
            dma(()),
            dma(()),
            dma(()),
            dma((groups,)),
            dma((2,)),
            dma((seq,)),
            dma(()),
            dma(()),
            dma(()),
            dma(()),
            dma(()),
            dma(()),
            dma(()),
            dma(()),
            dma(()),
            dma((groups, others)),
            dma(()),
            dma(()),
            dma((groups, others)),
        ],
        compiler_params=pltpu.CompilerParams(
            collective_id=0, has_side_effects=True, vmem_limit_bytes=60000000
        ),
    )(*operands)
    return pl.pallas_call(
        write_out,
        out_shape=shapes,
        in_specs=[whole] * 3,
        out_specs=(whole,) * 3,
        compiler_params=pltpu.CompilerParams(vmem_limit_bytes=8 * 2**20),
    )(*results)


def fits(mesh, operands):
    seq, tensor = mesh.shape["seq"], mesh.shape["tensor"]
    vq, weight, cq, aq = operands[0], operands[4], operands[5], operands[8]
    return (
        seq > 1
        and (vq.shape[1] // HD) % seq == 0
        and tensor % 2 == 0
        and (weight.shape[1] // tensor) % WIDE == 0
        and aq.shape[0] % 16 == 0
        and vq.shape[0] % 16 == 0
        and 2 * (cq.shape[1] // HD) <= HD
        and weight.size * 2 <= 10 * 2**20
        and vq.shape[0] <= 128
        and seq <= 8
    )


def solution(mesh):
    def step(*operands):
        if fits(mesh, operands):
            return fused(mesh.shape["seq"], mesh.shape["tensor"], *operands)
        return local(*operands)

    in_specs = (
        P(("groups", "seq"), "tensor"),
        P(("groups", "seq"), "tensor"),
        P(("groups", "seq"), "tensor"),
        P(("groups", "seq"), "tensor"),
        P("tensor", None),
        P(("groups", "seq"), "tensor"),
        P(("groups", "seq"), "tensor"),
        P(("groups", "seq"), "tensor"),
        P(("groups", "seq"), "tensor"),
        P(("groups", "seq"), "tensor"),
        P(("groups", "seq"), "tensor"),
    )
    out_specs = (
        P(("groups", "seq"), "tensor"),
        P(("groups", "seq"), "tensor"),
        P(("groups", "seq"), "tensor"),
    )
    return jax.shard_map(step, mesh=mesh, in_specs=in_specs, out_specs=out_specs, check_vma=False)
```

```python
import functools
import math

import jax
import jax.numpy as jnp
from jax import lax
from jax.experimental import pallas as pl
from jax.experimental.pallas import tpu as pltpu
from jax.sharding import PartitionSpec as P

HD = 128


def blank_state(query_rows, head_count):
    return (
        jnp.full((head_count, query_rows), -1e30, jnp.float32),
        jnp.zeros((head_count, query_rows), jnp.float32),
        jnp.zeros((head_count, query_rows, HD), jnp.float32),
    )


def absorb(carried, queries, keyset, values, head_count):
    running, row_sum, numerator = carried
    query_rows = queries.shape[0]
    key_rows = keyset.shape[0]
    factor = 1.0 / math.sqrt(HD)
    query_heads = queries.reshape(query_rows, head_count, HD)
    for offset in range(0, key_rows, 1024):
        width_keys = min(1024, key_rows - offset)
        key_block = keyset[offset : offset + width_keys].reshape(width_keys, head_count, HD)
        value_block = values[offset : offset + width_keys].reshape(width_keys, head_count, HD)
        scores = (
            jnp.einsum("qhd,khd->hqk", query_heads, key_block, preferred_element_type=jnp.float32)
            * factor
        )
        highest = jnp.maximum(running, jnp.max(scores, axis=2))
        raised = jnp.exp(scores - highest[:, :, None])
        shrink = jnp.exp(running - highest)
        row_sum = row_sum * shrink + jnp.sum(raised, axis=2)
        numerator = numerator * shrink[:, :, None] + jnp.einsum(
            "hqk,khd->hqd",
            raised.astype(jnp.bfloat16),
            value_block,
            preferred_element_type=jnp.float32,
        )
        running = highest
    return (running, row_sum, numerator)


def finish(carried, head_count):
    running, row_sum, numerator = carried
    result = numerator / row_sum[:, :, None]
    return result.transpose(1, 0, 2).reshape(result.shape[1], head_count * HD).astype(jnp.bfloat16)


def local(
    video_query,
    video_key,
    video_value,
    video_stream,
    out_weight,
    cross_query,
    audio_key,
    audio_value,
    audio_query,
    cross_key,
    cross_value,
):
    local_heads = video_query.shape[1] // HD
    query_rows = video_query.shape[0]
    pieces = (
        lax.all_gather(video_key, "seq", axis=0, tiled=True),
        lax.all_gather(video_value, "seq", axis=0, tiled=True),
    )
    carried_video = absorb(
        blank_state(query_rows, local_heads), video_query, pieces[0], pieces[1], local_heads
    )
    attended = finish(carried_video, local_heads)
    projected = jnp.dot(attended, out_weight, preferred_element_type=jnp.float32)
    summed = lax.psum_scatter(
        projected.astype(jnp.bfloat16), "tensor", scatter_dimension=1, tiled=True
    ).astype(jnp.float32)
    video_next = (video_stream.astype(jnp.float32) + summed).astype(jnp.bfloat16)
    cross_heads = cross_query.shape[1] // HD
    every_key, every_value = (
        lax.all_gather(audio_key, "seq", axis=0, tiled=True),
        lax.all_gather(audio_value, "seq", axis=0, tiled=True),
    )
    carried_audio = absorb(
        blank_state(cross_query.shape[0], cross_heads),
        cross_query,
        every_key,
        every_value,
        cross_heads,
    )
    video_cross = finish(carried_audio, cross_heads)
    pieces = (
        lax.all_gather(cross_key, "seq", axis=0, tiled=True),
        lax.all_gather(cross_value, "seq", axis=0, tiled=True),
    )
    carried_cross = absorb(
        blank_state(audio_query.shape[0], cross_heads),
        audio_query,
        pieces[0],
        pieces[1],
        cross_heads,
    )
    audio_cross = finish(carried_cross, cross_heads)
    return (video_next, video_cross, audio_cross)


MESH = pl.DeviceIdType.MESH
NT = (((1,), (1,)), ((), ()))
WIDE = 512
SHARES = (3, 3, 2)
SPLIT = True


def softmax_parts(queries, keyset, values):
    scores = lax.dot_general(queries, keyset, NT, preferred_element_type=jnp.float32) * (
        1.0 / math.sqrt(HD)
    )
    highest = jnp.max(scores, axis=1, keepdims=True)
    raised = jnp.exp(scores - highest)
    row_sum = jnp.sum(raised, axis=1, keepdims=True)
    numerator = jnp.dot(raised.astype(jnp.bfloat16), values, preferred_element_type=jnp.float32)
    return highest, row_sum, numerator


def row_cuts(rows):
    tiles, whole = rows // 16, sum(SHARES)
    marks = sorted({tiles * sum(SHARES[: i + 1]) // whole for i in range(len(SHARES))} | {0})
    return [(16 * a, 16 * (b - a)) for a, b in zip(marks, marks[1:])]


def by_distance(me, seq):
    right = (me < seq - 1 - me).astype(jnp.int32)
    toward = 2 * right - 1
    short = right * me + (1 - right) * (seq - 1 - me)
    order = []
    for i in range(seq - 1):
        both = (i < 2 * short).astype(jnp.int32)
        near = (i // 2 + 1) * (1 if i % 2 == 0 else -1)
        order.append(me + toward * (both * near + (1 - both) * (i - short + 1)))
    return order


def block_kernel(
    seq,
    tensor,
    vq,
    vk,
    vv,
    vs,
    weight,
    cq,
    ak,
    av,
    aq,
    ck,
    cv,
    next_ref,
    vcross_ref,
    across_ref,
    kv,
    q_all,
    heads_out,
    gathered,
    audio,
    partial,
    partial_in,
    cross_v,
    stream_v,
    weight_v,
    kept,
    mine,
    other,
    pair_out,
    pair_in,
    far_out,
    far_in,
    token,
    beside,
    kv_send,
    kv_recv,
    q_send,
    q_recv,
    own_kv,
    own_q,
    out_send,
    out_recv,
    out_last,
    audio_send,
    audio_recv,
    audio_own,
    part_send,
    part_recv,
    cross_sem,
    stream_sem,
    weight_sem,
    pair_send,
    pair_recv,
    home_recv,
    far_send,
    far_recv,
):
    rows = vq.shape[0]
    span = vq.shape[1] // seq
    share = span // HD
    cross_heads = cq.shape[1] // HD
    audio_rows = aq.shape[0]
    chips = tensor // 2
    width = next_ref.shape[1]
    pieces = width // WIDE
    cuts = row_cuts(rows)
    groups = len(cuts)
    me = lax.axis_index("seq")
    place = lax.axis_index("tensor")
    core = lax.rem(place, 2)
    chip = place // 2
    sibling = chip * 2 + (1 - core)
    peers = by_distance(me, seq)
    far_chips = [lax.rem(chip + d, chips) for d in range(chips)]

    def rows_of(p):
        return pl.ds(pl.multiple_of(p * rows, rows), rows)

    def audio_rows_of(p):
        return pl.ds(pl.multiple_of(p * audio_rows, audio_rows), audio_rows)

    def cols_of(p):
        return pl.ds(pl.multiple_of(p * span, span), span)

    def slot(p, r):
        start, size = cuts[r]
        return pl.ds(pl.multiple_of(seq * start + p * size, 16), size)

    for kind, ref in enumerate((vk, vv)):
        pltpu.make_async_copy(ref.at[:, cols_of(me)], kv.at[kind, rows_of(me)], own_kv).start()
    for r in range(groups):
        pltpu.make_async_copy(vq.at[pl.ds(*cuts[r]), cols_of(me)], q_all.at[slot(me, r)], own_q).start()
    for kind, ref in enumerate((ak, av, aq)):
        pltpu.make_async_copy(ref, audio.at[kind, audio_rows_of(me)], audio_own).start()
    for kind, ref in enumerate((cq, ck, cv)):
        pltpu.make_async_copy(ref, cross_v.at[kind], cross_sem).start()
    stream_copy = pltpu.make_async_copy(vs, stream_v, stream_sem)
    stream_copy.start()

    def local_done(ref, sem):
        pltpu.make_async_copy(ref, ref, sem).wait()

    barrier = pltpu.get_barrier_semaphore()
    for way in (1, -1):

        @pl.when((me + way >= 0) & (me + way < seq))
        def _():
            pl.semaphore_signal(barrier, inc=1, device_id={"seq": me + way}, device_id_type=MESH)

    pl.semaphore_signal(barrier, inc=1, device_id={"tensor": sibling}, device_id_type=MESH)
    for d in range(1, chips):
        pl.semaphore_signal(
            barrier, inc=1, device_id={"tensor": far_chips[d] * 2 + core}, device_id_type=MESH
        )
    inner = ((me > 0) & (me < seq - 1)).astype(jnp.int32)
    with jax.named_scope("barrier"):
        pl.semaphore_wait(barrier, chips + 1 + inner)

    def to_seq(src, dst, send_sem, recv_sem, p):
        return pltpu.make_async_remote_copy(
            src_ref=src,
            dst_ref=dst,
            send_sem=send_sem,
            recv_sem=recv_sem,
            device_id={"seq": p},
            device_id_type=MESH,
        )

    def all_of(ref, send_sem, recv_sem):
        return to_seq(ref, ref, send_sem, recv_sem, peers[0])

    def keys_to(p, kinds=(0, 1)):
        for kind, ref in zip(kinds, (vk, vv)[kinds[0] :]):
            to_seq(ref.at[:, cols_of(p)], kv.at[kind, rows_of(me)], kv_send, kv_recv.at[me], p).start()

    def send_queries(r):
        here = pl.ds(*cuts[r])
        for p in peers[::-1]:
            to_seq(vq.at[here, cols_of(p)], q_all.at[slot(me, r)], q_send, q_recv.at[r], p).start()

    def audio_hop(step, way, part):
        shard = lax.rem(me - way * step + seq, seq)
        here = audio_rows_of(shard)
        block = audio.at[2, here] if part else audio.at[pl.ds(0, 2), here]
        return to_seq(
            block,
            block,
            audio_send.at[part, (way + 1) // 2, step],
            audio_recv.at[part, shard],
            lax.rem(me + way + seq, seq),
        )

    def on_line(step, way):
        source, target = me - way * step, me + way
        return (source >= 0) & (source < seq) & (target >= 0) & (target < seq)

    def pass_audio(step, part):
        for way in (1, -1):

            @pl.when(on_line(step, way))
            def _():
                copy = audio_hop(step, way, part)
                if step:
                    copy.wait_recv()
                copy.start()

    def crosses(way):
        return me == (seq // 2 - 1 if way > 0 else seq // 2)

    def some_audio(steps, chosen):
        for step in steps:
            for way in (1, -1):

                @pl.when(on_line(step, way) & chosen(step, way))
                def _():
                    copy = audio_hop(step, way, 0)
                    if step:
                        copy.wait_recv()
                    copy.start()

    def early_part():
        some_audio((0,), lambda step, way: jnp.logical_not(crosses(way)))

    def cross_part():
        some_audio((0, 1), lambda step, way: crosses(way))

    def relay_part():
        some_audio(range(1, seq - 1), lambda step, way: (step > 1) | jnp.logical_not(crosses(way)))

    def end_audio(part):
        for step in range(1, seq):
            for way in (1, -1):
                source, target = me - way * step, me + way
                last = (target < 0) | (target >= seq)

                @pl.when((source >= 0) & (source < seq) & last)
                def _():
                    audio_hop(step, way, part).wait_recv()

    def token_to(way):
        pl.semaphore_signal(
            token.at[(way + 1) // 2], inc=1, device_id={"seq": me + way}, device_id_type=MESH
        )

    def within(p):
        return (p >= 0) & (p < seq)

    def first_tokens():
        for way in (1, -1):

            @pl.when(within(me - way) & jnp.logical_not(within(me - 2 * way)) & within(me + way))
            def _():
                token_to(way)

    def tokens():
        for way in (1, -1):

            @pl.when(within(me - 2 * way))
            def _():
                pl.semaphore_wait(token.at[(way + 1) // 2], 1)

            @pl.when(within(me - 2 * way) & within(me + way))
            def _():
                token_to(way)

    local_done(audio.at[:, audio_rows_of(0)], audio_own)
    def keys_from(p):
        all_of(kv.at[:, rows_of(0)], kv_send, kv_recv.at[p]).wait_recv()

    def first_keys():
        keys_from(peers[0])

    def run(name, f, *args):
        with jax.named_scope(name):
            f(*args)

    def late_audio(part):
        for step in range(2, seq - 1):
            pass_audio(step, part)

    def meet():
        pl.semaphore_signal(
            beside.at[0], inc=1, device_id={"tensor": sibling}, device_id_type=MESH
        )
        pl.semaphore_wait(beside.at[0], 1)

    run("p0", pass_audio, 0, 1)
    run("K0", keys_to, peers[0])
    run("tk1", first_tokens)
    run("tok", tokens)
    run("sib", meet)
    run("K1", keys_to, peers[1])
    run("K2", keys_to, peers[2])
    run("PE", early_part)
    run("p1", pass_audio, 1, 1)
    run("q0", send_queries, 0)
    weight_copy = pltpu.make_async_copy(weight, weight_v, weight_sem)
    weight_copy.start()

    def wait_keys():
        local_done(kv.at[:, rows_of(0)], own_kv)
        local_done(q_all.at[rows_of(0)], own_q)
        for p in peers[1:]:
            keys_from(p)

    def attend_rows(r):
        start, size = cuts[r]
        all_of(q_all.at[pl.ds(0, (seq - 1) * size)], q_send, q_recv.at[r]).wait_recv()
        block = pl.ds(seq * start, seq * size)
        for h in range(share):
            cols = slice(h * HD, (h + 1) * HD)
            _, row_sum, numerator = softmax_parts(q_all[block, cols], kv[0, :, cols], kv[1, :, cols])
            heads_out[block, cols] = (numerator / row_sum).astype(jnp.bfloat16)
        here = pl.ds(start, size)
        for p in peers[::-1]:
            sem = out_last.at[me] if SPLIT and r == groups - 1 else out_recv.at[r]
            to_seq(heads_out.at[slot(p, r)], gathered.at[me, here], out_send, sem, p).start()
        gathered[me, here] = heads_out[slot(me, r)]

    def upper(value):
        return value.astype(jnp.bfloat16).astype(jnp.float32)

    def cross_audio():
        local_done(cross_v, cross_sem)
        end_audio(1)
        lane = lax.broadcasted_iota(jnp.int32, (seq * audio_rows, HD), 1)
        held = jnp.zeros((seq * audio_rows, HD), jnp.float32)
        for c in range(cross_heads):
            cols = slice(c * HD, (c + 1) * HD)
            highest, row_sum, numerator = softmax_parts(
                audio[2, :, cols], cross_v[1, :, cols], cross_v[2, :, cols]
            )
            for i, value in enumerate((highest, row_sum)):
                held = jnp.where(lane == 2 * (2 * c + i), upper(value), held)
                held = jnp.where(lane == 2 * (2 * c + i) + 1, value - upper(value), held)
            partial[:, cols] = numerator.astype(jnp.bfloat16)
        partial[:, cross_heads * HD :] = held.astype(jnp.bfloat16)

    def cross_video():
        end_audio(0)
        for c in range(cross_heads):
            cols = slice(c * HD, (c + 1) * HD)
            _, row_sum, numerator = softmax_parts(
                cross_v[0, :, cols], audio[0, :, cols], audio[1, :, cols]
            )
            vcross_ref[:, cols] = (numerator / row_sum).astype(jnp.bfloat16)

    def cross_send():
        for p in peers:
            theirs = audio_rows_of(p)
            to_seq(partial.at[theirs], partial_in.at[me], part_send, part_recv, p).start()

    def cross_finish():
        all_of(partial_in.at[pl.ds(0, seq - 1)], part_send, part_recv).wait_recv()
        my_audio = audio_rows_of(me)
        stat_cols = slice(cross_heads * HD, (cross_heads + 1) * HD)
        held = [partial[my_audio, stat_cols]] + [partial_in[p, :, stat_cols] for p in peers]
        held = [value.astype(jnp.float32) for value in held]

        def stat(s, i):
            return s[:, 2 * i : 2 * i + 1] + s[:, 2 * i + 1 : 2 * i + 2]

        for c in range(cross_heads):
            cols = slice(c * HD, (c + 1) * HD)
            parts = [partial[my_audio, cols]] + [partial_in[p, :, cols] for p in peers]
            tops = [stat(s, 2 * c) for s in held]
            sums = [stat(s, 2 * c + 1) for s in held]
            highest = functools.reduce(jnp.maximum, tops)
            factors = [jnp.exp(t - highest) for t in tops]
            row_sum = sum(f * s for f, s in zip(factors, sums))
            numerator = sum(f * n.astype(jnp.float32) for f, n in zip(factors, parts))
            across_ref[:, cols] = (numerator / row_sum).astype(jnp.bfloat16)

    def product(attended, d, side, j):
        target = far_chips[d] * 2 + (core if side else 1 - core)
        cols = pl.ds(pl.multiple_of(target * width + j * WIDE, WIDE), WIDE)
        return jnp.dot(attended, weight_v[:, cols], preferred_element_type=jnp.float32)

    def pair_copy(r, d):
        here = pl.ds(*cuts[r])
        return pltpu.make_async_remote_copy(
            src_ref=pair_out.at[d, here],
            dst_ref=pair_in.at[d, here],
            send_sem=pair_send,
            recv_sem=pair_recv.at[r, d - 1],
            device_id={"tensor": sibling},
            device_id_type=MESH,
        )

    def far_copy(r, d):
        here = pl.ds(*cuts[r])
        return pltpu.make_async_remote_copy(
            src_ref=far_out.at[d - 1, here],
            dst_ref=far_in.at[d - 1, here],
            send_sem=far_send,
            recv_sem=far_recv.at[r, d - 1],
            device_id={"tensor": far_chips[d] * 2 + core},
            device_id_type=MESH,
        )

    home_copy = pltpu.make_async_remote_copy(
        src_ref=pair_out.at[0],
        dst_ref=pair_in.at[0],
        send_sem=pair_send,
        recv_sem=home_recv,
        device_id={"tensor": sibling},
        device_id_type=MESH,
    )
    blocks = [slice(j * WIDE, (j + 1) * WIDE) for j in range(pieces)]

    def share_rows(r):
        here = pl.ds(*cuts[r])
        all_of(gathered.at[pl.ds(0, seq - 1), here], out_send, out_recv.at[r]).wait_recv()
        attended = jnp.concatenate([gathered[p, here] for p in range(seq)], axis=1)
        if r == 0:
            weight_copy.wait()
        for d in range(1, chips):
            for j, block in enumerate(blocks):
                pair_out[d, here, block] = product(attended, d, 0, j).astype(jnp.bfloat16)
            pair_copy(r, d).start()
        for d in range(1, chips):
            for j, block in enumerate(blocks):
                mine[d - 1, here, block] = product(attended, d, 1, j)

    def share_parts(r):
        here = pl.ds(*cuts[r])

        def add_part(some, d, side, first):
            target = far_chips[d] * 2 + (core if side else 1 - core)
            for j, block in enumerate(blocks):
                cols = pl.ds(pl.multiple_of(target * width + j * WIDE, WIDE), WIDE)
                value = sum(
                    jnp.dot(gathered[p, here], weight_v[cols_of(p), cols], preferred_element_type=jnp.float32)
                    for p in some
                )
                ref = mine if side else other
                ref[d - 1, here, block] = value if first else ref[d - 1, here, block] + value

        some = [me]
        for i, p in enumerate(peers):
            all_of(gathered.at[0, here], out_send, out_last.at[p]).wait_recv()
            some.append(p)
            if i == 0 and len(peers) > 1:
                continue
            for side in (0, 1):
                for d in range(1, chips):
                    add_part(some, d, side, i <= 1)
                    if side == 0 and i == len(peers) - 1:
                        pair_out[d, here] = other[d - 1, here].astype(jnp.bfloat16)
                        pair_copy(r, d).start()
            some = []

    def send_far(r):
        here = pl.ds(*cuts[r])
        for d in range(1, chips):
            pair_copy(r, d).wait_recv()
            far_out[d - 1, here] = (mine[d - 1, here] + pair_in[d, here].astype(jnp.float32)).astype(
                jnp.bfloat16
            )
            far_copy(r, d).start()

    def all_heads():
        return jnp.concatenate([gathered[p] for p in range(seq)], axis=1)

    def give_home():
        attended = all_heads()
        for j, block in enumerate(blocks):
            pair_out[0, :, block] = product(attended, 0, 0, j).astype(jnp.bfloat16)
        home_copy.start()

    def keep_home():
        attended = all_heads()
        stream_copy.wait()
        for j, block in enumerate(blocks):
            kept[:, block] = product(attended, 0, 1, j) + stream_v[:, block].astype(jnp.float32)

    def close_rows(r):
        here = pl.ds(*cuts[r])
        value = kept[here] + pair_in[0, here].astype(jnp.float32)
        for d in range(1, chips):
            far_copy(r, d).wait_recv()
            value = value + far_in[d - 1, here].astype(jnp.float32)
        next_ref[here] = value.astype(jnp.bfloat16)

    def settle():
        all_of(kv.at[:, pl.ds(0, (seq - 1) * rows)], kv_send, kv_recv.at[0]).wait_send()
        all_of(q_all.at[pl.ds(0, (seq - 1) * rows)], q_send, q_recv.at[0]).wait_send()
        all_of(heads_out.at[pl.ds(0, (seq - 1) * rows)], out_send, out_recv.at[0]).wait_send()
        all_of(partial.at[pl.ds(0, (seq - 1) * audio_rows)], part_send, part_recv).wait_send()
        for way in (1, -1):
            for step in range(seq - 1):

                @pl.when(on_line(step, way))
                def _():
                    for part in (0, 1):
                        audio_hop(step, way, part).wait_send()

        all_of(pair_out, pair_send, pair_recv.at[0, 0]).wait_send()
        if chips > 1:
            all_of(far_out, far_send, far_recv.at[0, 0]).wait_send()

    run("w0", first_keys)
    run("wk", wait_keys)
    run("q1", send_queries, 1)
    run("p2", late_audio, 1)
    run("a0", attend_rows, 0)
    run("q2", send_queries, 2)
    run("a1", attend_rows, 1)
    run("ca", cross_audio)
    run("A0", share_rows, 0)
    run("a2", attend_rows, 2)
    run("PL", cross_part)
    run("B0", send_far, 0)
    run("A1", share_rows, 1)
    run("B1", send_far, 1)
    run("cs", cross_send)
    run("PR", relay_part)
    run("A2", share_parts, 2)
    run("B2", send_far, 2)
    run("k0", give_home)
    run("k1", keep_home)
    run("cf", cross_finish)
    run("cv", cross_video)
    run("h", home_copy.wait_recv)
    run("c0", close_rows, 0)
    run("c1", close_rows, 1)
    run("c2", close_rows, 2)
    with jax.named_scope("settle"):
        settle()


def write_out(*refs):
    half = len(refs) // 2
    for src, dst in zip(refs[:half], refs[half:]):
        dst[...] = src[...]


def fused(seq, tensor, *operands):
    vq, vk, vv, vs, weight, cq, ak, av, aq, ck, cv = operands
    rows, features = vq.shape
    span = features // seq
    audio_rows, cross_width = aq.shape
    chips = tensor // 2
    width = weight.shape[1] // tensor
    groups = len(row_cuts(rows))
    others = max(chips - 1, 1)
    bf16, f32, dma = jnp.bfloat16, jnp.float32, pltpu.SemaphoreType.DMA
    shapes = tuple(jax.ShapeDtypeStruct(x.shape, bf16) for x in (vs, cq, aq))
    whole = pl.BlockSpec(memory_space=pltpu.VMEM)
    results = pl.pallas_call(
        functools.partial(block_kernel, seq, tensor),
        out_shape=tuple(pltpu.VMEM(x.shape, bf16) for x in (vs, cq, aq)),
        in_specs=[pl.BlockSpec(memory_space=pltpu.HBM)] * 11,
        out_specs=(whole,) * 3,
        scratch_shapes=[
            pltpu.VMEM((2, seq * rows, span), bf16),
            pltpu.VMEM((seq * rows, span), bf16),
            pltpu.VMEM((seq * rows, span), bf16),
            pltpu.VMEM((seq, rows, span), bf16),
            pltpu.VMEM((3, seq * audio_rows, cross_width), bf16),
            pltpu.VMEM((seq * audio_rows, cross_width + HD), bf16),
            pltpu.VMEM((seq, audio_rows, cross_width + HD), bf16),
            pltpu.VMEM((3, *cq.shape), bf16),
            pltpu.VMEM(vs.shape, bf16),
            pltpu.VMEM(weight.shape, bf16),
            pltpu.VMEM(vs.shape, f32),
            pltpu.VMEM((others, rows, width), f32),
            pltpu.VMEM((others, rows, width), f32),
            pltpu.VMEM((chips, rows, width), bf16),
            pltpu.VMEM((chips, rows, width), bf16),
            pltpu.VMEM((others, rows, width), bf16),
            pltpu.VMEM((others, rows, width), bf16),
            pltpu.SemaphoreType.REGULAR((2,)),
            pltpu.SemaphoreType.REGULAR((1,)),
            dma(()),
            dma((seq,)),
            dma(()),
            dma((groups,)),
            dma(()),
            dma(()),
            dma(()),
            dma((groups,)),
            dma((seq,)),
            dma((2, 2, seq - 1)),
            dma((2, seq)),
            dma(()),
            dma(()),
            dma(()),
            dma(()),
            dma(()),
            dma(()),
            dma(()),
            dma((groups, others)),
            dma(()),
            dma(()),
            dma((groups, others)),
        ],
        compiler_params=pltpu.CompilerParams(
            collective_id=0, has_side_effects=True, vmem_limit_bytes=60000000
        ),
    )(*operands)
    return pl.pallas_call(
        write_out,
        out_shape=shapes,
        in_specs=[whole] * 3,
        out_specs=(whole,) * 3,
        compiler_params=pltpu.CompilerParams(vmem_limit_bytes=8 * 2**20),
    )(*results)


def fits(mesh, operands):
    seq, tensor = mesh.shape["seq"], mesh.shape["tensor"]
    vq, weight, cq, aq = operands[0], operands[4], operands[5], operands[8]
    return (
        seq > 1
        and (vq.shape[1] // HD) % seq == 0
        and tensor % 2 == 0
        and (weight.shape[1] // tensor) % WIDE == 0
        and aq.shape[0] % 16 == 0
        and vq.shape[0] % 16 == 0
        and 4 * (cq.shape[1] // HD) <= HD
        and weight.size * 2 <= 10 * 2**20
        and vq.shape[0] <= 128
        and seq <= 8
    )


def solution(mesh):
    def step(*operands):
        if fits(mesh, operands):
            return fused(mesh.shape["seq"], mesh.shape["tensor"], *operands)
        return local(*operands)

    in_specs = (
        P(("groups", "seq"), "tensor"),
        P(("groups", "seq"), "tensor"),
        P(("groups", "seq"), "tensor"),
        P(("groups", "seq"), "tensor"),
        P("tensor", None),
        P(("groups", "seq"), "tensor"),
        P(("groups", "seq"), "tensor"),
        P(("groups", "seq"), "tensor"),
        P(("groups", "seq"), "tensor"),
        P(("groups", "seq"), "tensor"),
        P(("groups", "seq"), "tensor"),
    )
    out_specs = (
        P(("groups", "seq"), "tensor"),
        P(("groups", "seq"), "tensor"),
        P(("groups", "seq"), "tensor"),
    )
    return jax.shard_map(step, mesh=mesh, in_specs=in_specs, out_specs=out_specs, check_vma=False)
```

```python
import functools
import math

import jax
import jax.numpy as jnp
from jax import lax
from jax.experimental import pallas as pl
from jax.experimental.pallas import tpu as pltpu
from jax.sharding import PartitionSpec as P

HD = 128


def blank_state(query_rows, head_count):
    return (
        jnp.full((head_count, query_rows), -1e30, jnp.float32),
        jnp.zeros((head_count, query_rows), jnp.float32),
        jnp.zeros((head_count, query_rows, HD), jnp.float32),
    )


def absorb(carried, queries, keyset, values, head_count):
    running, row_sum, numerator = carried
    query_rows = queries.shape[0]
    key_rows = keyset.shape[0]
    factor = 1.0 / math.sqrt(HD)
    query_heads = queries.reshape(query_rows, head_count, HD)
    for offset in range(0, key_rows, 1024):
        width_keys = min(1024, key_rows - offset)
        key_block = keyset[offset : offset + width_keys].reshape(width_keys, head_count, HD)
        value_block = values[offset : offset + width_keys].reshape(width_keys, head_count, HD)
        scores = (
            jnp.einsum("qhd,khd->hqk", query_heads, key_block, preferred_element_type=jnp.float32)
            * factor
        )
        highest = jnp.maximum(running, jnp.max(scores, axis=2))
        raised = jnp.exp(scores - highest[:, :, None])
        shrink = jnp.exp(running - highest)
        row_sum = row_sum * shrink + jnp.sum(raised, axis=2)
        numerator = numerator * shrink[:, :, None] + jnp.einsum(
            "hqk,khd->hqd",
            raised.astype(jnp.bfloat16),
            value_block,
            preferred_element_type=jnp.float32,
        )
        running = highest
    return (running, row_sum, numerator)


def finish(carried, head_count):
    running, row_sum, numerator = carried
    result = numerator / row_sum[:, :, None]
    return result.transpose(1, 0, 2).reshape(result.shape[1], head_count * HD).astype(jnp.bfloat16)


def local(
    video_query,
    video_key,
    video_value,
    video_stream,
    out_weight,
    cross_query,
    audio_key,
    audio_value,
    audio_query,
    cross_key,
    cross_value,
):
    local_heads = video_query.shape[1] // HD
    query_rows = video_query.shape[0]
    pieces = (
        lax.all_gather(video_key, "seq", axis=0, tiled=True),
        lax.all_gather(video_value, "seq", axis=0, tiled=True),
    )
    carried_video = absorb(
        blank_state(query_rows, local_heads), video_query, pieces[0], pieces[1], local_heads
    )
    attended = finish(carried_video, local_heads)
    projected = jnp.dot(attended, out_weight, preferred_element_type=jnp.float32)
    summed = lax.psum_scatter(
        projected.astype(jnp.bfloat16), "tensor", scatter_dimension=1, tiled=True
    ).astype(jnp.float32)
    video_next = (video_stream.astype(jnp.float32) + summed).astype(jnp.bfloat16)
    cross_heads = cross_query.shape[1] // HD
    every_key, every_value = (
        lax.all_gather(audio_key, "seq", axis=0, tiled=True),
        lax.all_gather(audio_value, "seq", axis=0, tiled=True),
    )
    carried_audio = absorb(
        blank_state(cross_query.shape[0], cross_heads),
        cross_query,
        every_key,
        every_value,
        cross_heads,
    )
    video_cross = finish(carried_audio, cross_heads)
    pieces = (
        lax.all_gather(cross_key, "seq", axis=0, tiled=True),
        lax.all_gather(cross_value, "seq", axis=0, tiled=True),
    )
    carried_cross = absorb(
        blank_state(audio_query.shape[0], cross_heads),
        audio_query,
        pieces[0],
        pieces[1],
        cross_heads,
    )
    audio_cross = finish(carried_cross, cross_heads)
    return (video_next, video_cross, audio_cross)


MESH = pl.DeviceIdType.MESH
NT = (((1,), (1,)), ((), ()))
WIDE = 512
SHARES = (4, 3, 1)
SPLIT = True


def softmax_parts(queries, keyset, values):
    scores = lax.dot_general(queries, keyset, NT, preferred_element_type=jnp.float32) * (
        1.0 / math.sqrt(HD)
    )
    highest = jnp.max(scores, axis=1, keepdims=True)
    raised = jnp.exp(scores - highest)
    row_sum = jnp.sum(raised, axis=1, keepdims=True)
    numerator = jnp.dot(raised.astype(jnp.bfloat16), values, preferred_element_type=jnp.float32)
    return highest, row_sum, numerator


def row_cuts(rows):
    tiles, whole = rows // 16, sum(SHARES)
    marks = sorted({tiles * sum(SHARES[: i + 1]) // whole for i in range(len(SHARES))} | {0})
    return [(16 * a, 16 * (b - a)) for a, b in zip(marks, marks[1:])]


def by_distance(me, seq):
    right = (me < seq - 1 - me).astype(jnp.int32)
    toward = 2 * right - 1
    short = right * me + (1 - right) * (seq - 1 - me)
    order = []
    for i in range(seq - 1):
        both = (i < 2 * short).astype(jnp.int32)
        near = (i // 2 + 1) * (1 if i % 2 == 0 else -1)
        order.append(me + toward * (both * near + (1 - both) * (i - short + 1)))
    return order


def block_kernel(
    seq,
    tensor,
    vq,
    vk,
    vv,
    vs,
    weight,
    cq,
    ak,
    av,
    aq,
    ck,
    cv,
    next_ref,
    vcross_ref,
    across_ref,
    kv,
    q_all,
    heads_out,
    gathered,
    audio,
    partial,
    partial_in,
    cross_v,
    stream_v,
    weight_v,
    kept,
    mine,
    other,
    pair_out,
    pair_in,
    far_out,
    far_in,
    token,
    beside,
    kv_send,
    kv_recv,
    q_send,
    q_recv,
    own_sem,
    out_send,
    out_recv,
    out_last,
    audio_send,
    audio_recv,
    audio_own,
    part_send,
    part_recv,
    cross_sem,
    stream_sem,
    weight_sem,
    pair_send,
    pair_recv,
    home_recv,
    far_send,
    far_recv,
):
    rows = vq.shape[0]
    span = vq.shape[1] // seq
    share = span // HD
    cross_heads = cq.shape[1] // HD
    audio_rows, cross_width = aq.shape
    chips = tensor // 2
    width = next_ref.shape[1]
    pieces = width // WIDE
    cuts = row_cuts(rows)
    groups = len(cuts)
    me = lax.axis_index("seq")
    place = lax.axis_index("tensor")
    core = lax.rem(place, 2)
    chip = place // 2
    sibling = chip * 2 + (1 - core)
    peers = by_distance(me, seq)
    far_chips = [lax.rem(chip + d, chips) for d in range(chips)]

    def rows_of(p):
        return pl.ds(pl.multiple_of(p * rows, rows), rows)

    def audio_rows_of(p):
        return pl.ds(pl.multiple_of(p * audio_rows, audio_rows), audio_rows)

    def cols_of(p):
        return pl.ds(pl.multiple_of(p * span, span), span)

    def slot(p, r):
        start, size = cuts[r]
        return pl.ds(pl.multiple_of(seq * start + p * size, 16), size)

    for kind, ref in enumerate((vk, vv)):
        pltpu.make_async_copy(ref.at[:, cols_of(me)], kv.at[kind, rows_of(me)], own_sem).start()
    for r in range(groups):
        pltpu.make_async_copy(vq.at[pl.ds(*cuts[r]), cols_of(me)], q_all.at[slot(me, r)], own_sem).start()
    for kind, ref in enumerate((ak, av, aq)):
        pltpu.make_async_copy(ref, audio.at[kind, audio_rows_of(me)], audio_own).start()
    for kind, ref in enumerate((cq, ck, cv)):
        pltpu.make_async_copy(ref, cross_v.at[kind], cross_sem).start()
    stream_copy = pltpu.make_async_copy(vs, stream_v, stream_sem)
    stream_copy.start()

    def local_done(ref, sem):
        pltpu.make_async_copy(ref, ref, sem).wait()

    barrier = pltpu.get_barrier_semaphore()
    for way in (1, -1):

        @pl.when((me + way >= 0) & (me + way < seq))
        def _():
            pl.semaphore_signal(barrier, inc=1, device_id={"seq": me + way}, device_id_type=MESH)

    pl.semaphore_signal(barrier, inc=1, device_id={"tensor": sibling}, device_id_type=MESH)
    for d in range(1, chips):
        pl.semaphore_signal(
            barrier, inc=1, device_id={"tensor": far_chips[d] * 2 + core}, device_id_type=MESH
        )
    inner = ((me > 0) & (me < seq - 1)).astype(jnp.int32)
    with jax.named_scope("barrier"):
        pl.semaphore_wait(barrier, chips + 1 + inner)

    def to_seq(src, dst, send_sem, recv_sem, p):
        return pltpu.make_async_remote_copy(
            src_ref=src,
            dst_ref=dst,
            send_sem=send_sem,
            recv_sem=recv_sem,
            device_id={"seq": p},
            device_id_type=MESH,
        )

    def all_of(ref, send_sem, recv_sem):
        return to_seq(ref, ref, send_sem, recv_sem, peers[0])

    def keys_to(p, kinds=(0, 1)):
        for kind, ref in zip(kinds, (vk, vv)[kinds[0] :]):
            to_seq(ref.at[:, cols_of(p)], kv.at[kind, rows_of(me)], kv_send, kv_recv, p).start()

    def send_queries(r):
        here = pl.ds(*cuts[r])
        for p in peers[::-1]:
            to_seq(vq.at[here, cols_of(p)], q_all.at[slot(me, r)], q_send, q_recv.at[r], p).start()

    def audio_hop(step, way, part):
        shard = lax.rem(me - way * step + seq, seq)
        here = audio_rows_of(shard)
        block = audio.at[2, here] if part else audio.at[pl.ds(0, 2), here]
        return to_seq(
            block,
            block,
            audio_send.at[part],
            audio_recv.at[part, shard],
            lax.rem(me + way + seq, seq),
        )

    def on_line(step, way):
        source, target = me - way * step, me + way
        return (source >= 0) & (source < seq) & (target >= 0) & (target < seq)

    def pass_audio(step, part):
        for way in (1, -1):

            @pl.when(on_line(step, way))
            def _():
                copy = audio_hop(step, way, part)
                if step:
                    copy.wait_recv()
                copy.start()

    def crosses(way):
        return me == (seq // 2 - 1 if way > 0 else seq // 2)

    def some_audio(steps, chosen):
        for step in steps:
            for way in (1, -1):

                @pl.when(on_line(step, way) & chosen(step, way))
                def _():
                    copy = audio_hop(step, way, 0)
                    if step:
                        copy.wait_recv()
                    copy.start()

    def early_part():
        some_audio((0,), lambda step, way: jnp.logical_not(crosses(way)))

    def cross_part():
        some_audio((0, 1), lambda step, way: crosses(way))

    def relay_part():
        some_audio(range(1, seq - 1), lambda step, way: (step > 1) | jnp.logical_not(crosses(way)))

    def end_audio(part):
        for step in range(1, seq):
            for way in (1, -1):
                source, target = me - way * step, me + way
                last = (target < 0) | (target >= seq)

                @pl.when((source >= 0) & (source < seq) & last)
                def _():
                    audio_hop(step, way, part).wait_recv()

    def token_to(way):
        pl.semaphore_signal(
            token.at[(way + 1) // 2], inc=1, device_id={"seq": me + way}, device_id_type=MESH
        )

    def within(p):
        return (p >= 0) & (p < seq)

    def first_tokens():
        for way in (1, -1):

            @pl.when(within(me - way) & jnp.logical_not(within(me - 2 * way)) & within(me + way))
            def _():
                token_to(way)

    def tokens():
        for way in (1, -1):

            @pl.when(within(me - 2 * way))
            def _():
                pl.semaphore_wait(token.at[(way + 1) // 2], 1)

            @pl.when(within(me - 2 * way) & within(me + way))
            def _():
                token_to(way)

    local_done(audio.at[:, audio_rows_of(0)], audio_own)
    def run(name, f, *args):
        with jax.named_scope(name):
            f(*args)

    def late_audio(part):
        for step in range(2, seq - 1):
            pass_audio(step, part)

    def meet():
        pl.semaphore_signal(
            beside.at[0], inc=1, device_id={"tensor": sibling}, device_id_type=MESH
        )
        pl.semaphore_wait(beside.at[0], 1)

    run("p0", pass_audio, 0, 1)
    run("K0", keys_to, peers[0])
    run("tk1", first_tokens)
    run("tok", tokens)
    run("sib", meet)
    run("K1", keys_to, peers[1])
    run("K2", keys_to, peers[2])
    run("q0", send_queries, 0)
    run("PE", early_part)
    run("p1", pass_audio, 1, 1)
    weight_copy = pltpu.make_async_copy(weight, weight_v, weight_sem)
    weight_copy.start()

    def wait_keys():
        local_done(kv.at[:, pl.ds(0, rows * 3 // 2)], own_sem)
        all_of(kv.at[:, pl.ds(0, (seq - 1) * rows)], kv_send, kv_recv).wait_recv()

    def attend_rows(r):
        start, size = cuts[r]
        all_of(q_all.at[pl.ds(0, (seq - 1) * size)], q_send, q_recv.at[r]).wait_recv()
        block = pl.ds(seq * start, seq * size)
        for h in range(share):
            cols = slice(h * HD, (h + 1) * HD)
            _, row_sum, numerator = softmax_parts(q_all[block, cols], kv[0, :, cols], kv[1, :, cols])
            heads_out[block, cols] = (numerator / row_sum).astype(jnp.bfloat16)
        here = pl.ds(start, size)
        for p in peers[::-1]:
            sem = out_last.at[me] if SPLIT and r == groups - 1 else out_recv.at[r]
            to_seq(heads_out.at[slot(p, r)], gathered.at[me, here], out_send, sem, p).start()
        gathered[me, here] = heads_out[slot(me, r)]

    def upper(value):
        return value.astype(jnp.bfloat16).astype(jnp.float32)

    def cross_audio():
        local_done(cross_v, cross_sem)
        end_audio(1)
        lane = lax.broadcasted_iota(jnp.int32, (seq * audio_rows, HD), 1)
        held = jnp.zeros((seq * audio_rows, HD), jnp.float32)
        for c in range(cross_heads):
            cols = slice(c * HD, (c + 1) * HD)
            highest, row_sum, numerator = softmax_parts(
                audio[2, :, cols], cross_v[1, :, cols], cross_v[2, :, cols]
            )
            for i, value in enumerate((highest, row_sum)):
                held = jnp.where(lane == 2 * (2 * c + i), upper(value), held)
                held = jnp.where(lane == 2 * (2 * c + i) + 1, value - upper(value), held)
            partial[:, cols] = numerator.astype(jnp.bfloat16)
        partial[:, cross_heads * HD :] = held.astype(jnp.bfloat16)

    def cross_video():
        end_audio(0)
        for c in range(cross_heads):
            cols = slice(c * HD, (c + 1) * HD)
            _, row_sum, numerator = softmax_parts(
                cross_v[0, :, cols], audio[0, :, cols], audio[1, :, cols]
            )
            vcross_ref[:, cols] = (numerator / row_sum).astype(jnp.bfloat16)

    def cross_send():
        for p in peers:
            theirs = audio_rows_of(p)
            to_seq(partial.at[theirs], partial_in.at[me], part_send, part_recv, p).start()

    def cross_finish():
        all_of(partial_in.at[pl.ds(0, seq - 1)], part_send, part_recv).wait_recv()
        my_audio = audio_rows_of(me)
        stat_cols = slice(cross_heads * HD, (cross_heads + 1) * HD)
        held = [partial[my_audio, stat_cols]] + [partial_in[p, :, stat_cols] for p in peers]
        held = [value.astype(jnp.float32) for value in held]

        def stat(s, i):
            return s[:, 2 * i : 2 * i + 1] + s[:, 2 * i + 1 : 2 * i + 2]

        for c in range(cross_heads):
            cols = slice(c * HD, (c + 1) * HD)
            parts = [partial[my_audio, cols]] + [partial_in[p, :, cols] for p in peers]
            tops = [stat(s, 2 * c) for s in held]
            sums = [stat(s, 2 * c + 1) for s in held]
            highest = functools.reduce(jnp.maximum, tops)
            factors = [jnp.exp(t - highest) for t in tops]
            row_sum = sum(f * s for f, s in zip(factors, sums))
            numerator = sum(f * n.astype(jnp.float32) for f, n in zip(factors, parts))
            across_ref[:, cols] = (numerator / row_sum).astype(jnp.bfloat16)

    def product(attended, d, side, j):
        target = far_chips[d] * 2 + (core if side else 1 - core)
        cols = pl.ds(pl.multiple_of(target * width + j * WIDE, WIDE), WIDE)
        return jnp.dot(attended, weight_v[:, cols], preferred_element_type=jnp.float32)

    def pair_copy(r, d):
        here = pl.ds(*cuts[r])
        return pltpu.make_async_remote_copy(
            src_ref=pair_out.at[d, here],
            dst_ref=pair_in.at[d, here],
            send_sem=pair_send,
            recv_sem=pair_recv.at[r, d - 1],
            device_id={"tensor": sibling},
            device_id_type=MESH,
        )

    def far_copy(r, d):
        here = pl.ds(*cuts[r])
        return pltpu.make_async_remote_copy(
            src_ref=far_out.at[d - 1, here],
            dst_ref=far_in.at[d - 1, here],
            send_sem=far_send,
            recv_sem=far_recv.at[r, d - 1],
            device_id={"tensor": far_chips[d] * 2 + core},
            device_id_type=MESH,
        )

    home_copy = pltpu.make_async_remote_copy(
        src_ref=pair_out.at[0],
        dst_ref=pair_in.at[0],
        send_sem=pair_send,
        recv_sem=home_recv,
        device_id={"tensor": sibling},
        device_id_type=MESH,
    )
    blocks = [slice(j * WIDE, (j + 1) * WIDE) for j in range(pieces)]

    def share_rows(r):
        here = pl.ds(*cuts[r])
        all_of(gathered.at[pl.ds(0, seq - 1), here], out_send, out_recv.at[r]).wait_recv()
        attended = jnp.concatenate([gathered[p, here] for p in range(seq)], axis=1)
        if r == 0:
            weight_copy.wait()
        for d in range(1, chips):
            for j, block in enumerate(blocks):
                pair_out[d, here, block] = product(attended, d, 0, j).astype(jnp.bfloat16)
            pair_copy(r, d).start()
        for d in range(1, chips):
            for j, block in enumerate(blocks):
                mine[d - 1, here, block] = product(attended, d, 1, j)

    def share_parts(r):
        here = pl.ds(*cuts[r])

        def add_part(some, d, side, first):
            target = far_chips[d] * 2 + (core if side else 1 - core)
            for j, block in enumerate(blocks):
                cols = pl.ds(pl.multiple_of(target * width + j * WIDE, WIDE), WIDE)
                value = sum(
                    jnp.dot(gathered[p, here], weight_v[cols_of(p), cols], preferred_element_type=jnp.float32)
                    for p in some
                )
                ref = mine if side else other
                ref[d - 1, here, block] = value if first else ref[d - 1, here, block] + value

        some = [me]
        for i, p in enumerate(peers):
            all_of(gathered.at[0, here], out_send, out_last.at[p]).wait_recv()
            some.append(p)
            if i == 0 and len(peers) > 1:
                continue
            for side in (0, 1):
                for d in range(1, chips):
                    add_part(some, d, side, i <= 1)
                    if side == 0 and i == len(peers) - 1:
                        pair_out[d, here] = other[d - 1, here].astype(jnp.bfloat16)
                        pair_copy(r, d).start()
            some = []

    def send_far(r):
        here = pl.ds(*cuts[r])
        for d in range(1, chips):
            pair_copy(r, d).wait_recv()
            far_out[d - 1, here] = (mine[d - 1, here] + pair_in[d, here].astype(jnp.float32)).astype(
                jnp.bfloat16
            )
            far_copy(r, d).start()

    def all_heads():
        return jnp.concatenate([gathered[p] for p in range(seq)], axis=1)

    def give_home():
        attended = all_heads()
        for j, block in enumerate(blocks):
            pair_out[0, :, block] = product(attended, 0, 0, j).astype(jnp.bfloat16)
        home_copy.start()

    def keep_home():
        attended = all_heads()
        stream_copy.wait()
        for j, block in enumerate(blocks):
            kept[:, block] = product(attended, 0, 1, j) + stream_v[:, block].astype(jnp.float32)

    def close_rows(r):
        here = pl.ds(*cuts[r])
        value = kept[here] + pair_in[0, here].astype(jnp.float32)
        for d in range(1, chips):
            far_copy(r, d).wait_recv()
            value = value + far_in[d - 1, here].astype(jnp.float32)
        next_ref[here] = value.astype(jnp.bfloat16)

    def settle():
        all_of(kv.at[:, pl.ds(0, (seq - 1) * rows)], kv_send, kv_recv).wait_send()
        all_of(q_all.at[pl.ds(0, (seq - 1) * rows)], q_send, q_recv.at[0]).wait_send()
        all_of(heads_out.at[pl.ds(0, (seq - 1) * rows)], out_send, out_recv.at[0]).wait_send()
        all_of(partial.at[pl.ds(0, (seq - 1) * audio_rows)], part_send, part_recv).wait_send()
        block = audio_rows * cross_width // span
        for part, count in ((0, 2), (1, 1)):
            for hops, place_fits in ((1, inner == 0), (seq + 1, inner == 1)):

                @pl.when(place_fits)
                def _():
                    some = heads_out.at[pl.ds(0, hops * count * block)]
                    all_of(some, audio_send.at[part], audio_recv.at[part, 0]).wait_send()

        all_of(pair_out, pair_send, pair_recv.at[0, 0]).wait_send()
        if chips > 1:
            all_of(far_out, far_send, far_recv.at[0, 0]).wait_send()

    run("wk", wait_keys)
    run("q1", send_queries, 1)
    run("p2", late_audio, 1)
    run("a0", attend_rows, 0)
    run("q2", send_queries, 2)
    run("a1", attend_rows, 1)
    run("ca", cross_audio)
    run("A0", share_rows, 0)
    run("PL", cross_part)
    run("a2", attend_rows, 2)
    run("B0", send_far, 0)
    run("A1", share_rows, 1)
    run("B1", send_far, 1)
    run("cs", cross_send)
    run("PR", relay_part)
    run("A2", share_parts, 2)
    run("B2", send_far, 2)
    run("k0", give_home)
    run("k1", keep_home)
    run("cf", cross_finish)
    run("cv", cross_video)
    run("h", home_copy.wait_recv)
    run("c0", close_rows, 0)
    run("c1", close_rows, 1)
    run("c2", close_rows, 2)
    with jax.named_scope("settle"):
        settle()


def write_out(*refs):
    half = len(refs) // 2
    for src, dst in zip(refs[:half], refs[half:]):
        dst[...] = src[...]


def fused(seq, tensor, *operands):
    vq, vk, vv, vs, weight, cq, ak, av, aq, ck, cv = operands
    rows, features = vq.shape
    span = features // seq
    audio_rows, cross_width = aq.shape
    chips = tensor // 2
    width = weight.shape[1] // tensor
    groups = len(row_cuts(rows))
    others = max(chips - 1, 1)
    bf16, f32, dma = jnp.bfloat16, jnp.float32, pltpu.SemaphoreType.DMA
    shapes = tuple(jax.ShapeDtypeStruct(x.shape, bf16) for x in (vs, cq, aq))
    whole = pl.BlockSpec(memory_space=pltpu.VMEM)
    results = pl.pallas_call(
        functools.partial(block_kernel, seq, tensor),
        out_shape=tuple(pltpu.VMEM(x.shape, bf16) for x in (vs, cq, aq)),
        in_specs=[pl.BlockSpec(memory_space=pltpu.HBM)] * 11,
        out_specs=(whole,) * 3,
        scratch_shapes=[
            pltpu.VMEM((2, seq * rows, span), bf16),
            pltpu.VMEM((seq * rows, span), bf16),
            pltpu.VMEM((seq * rows, span), bf16),
            pltpu.VMEM((seq, rows, span), bf16),
            pltpu.VMEM((3, seq * audio_rows, cross_width), bf16),
            pltpu.VMEM((seq * audio_rows, cross_width + HD), bf16),
            pltpu.VMEM((seq, audio_rows, cross_width + HD), bf16),
            pltpu.VMEM((3, *cq.shape), bf16),
            pltpu.VMEM(vs.shape, bf16),
            pltpu.VMEM(weight.shape, bf16),
            pltpu.VMEM(vs.shape, f32),
            pltpu.VMEM((others, rows, width), f32),
            pltpu.VMEM((others, rows, width), f32),
            pltpu.VMEM((chips, rows, width), bf16),
            pltpu.VMEM((chips, rows, width), bf16),
            pltpu.VMEM((others, rows, width), bf16),
            pltpu.VMEM((others, rows, width), bf16),
            pltpu.SemaphoreType.REGULAR((2,)),
            pltpu.SemaphoreType.REGULAR((1,)),
            dma(()),
            dma(()),
            dma(()),
            dma((groups,)),
            dma(()),
            dma(()),
            dma((groups,)),
            dma((seq,)),
            dma((2,)),
            dma((2, seq)),
            dma(()),
            dma(()),
            dma(()),
            dma(()),
            dma(()),
            dma(()),
            dma(()),
            dma((groups, others)),
            dma(()),
            dma(()),
            dma((groups, others)),
        ],
        compiler_params=pltpu.CompilerParams(
            collective_id=0, has_side_effects=True, vmem_limit_bytes=60000000
        ),
    )(*operands)
    return pl.pallas_call(
        write_out,
        out_shape=shapes,
        in_specs=[whole] * 3,
        out_specs=(whole,) * 3,
        compiler_params=pltpu.CompilerParams(vmem_limit_bytes=8 * 2**20),
    )(*results)


def fits(mesh, operands):
    seq, tensor = mesh.shape["seq"], mesh.shape["tensor"]
    vq, weight, cq, aq = operands[0], operands[4], operands[5], operands[8]
    return (
        seq > 1
        and (vq.shape[1] // HD) % seq == 0
        and tensor % 2 == 0
        and (weight.shape[1] // tensor) % WIDE == 0
        and aq.shape[0] % 16 == 0
        and vq.shape[0] % 16 == 0
        and 4 * (cq.shape[1] // HD) <= HD
        and (aq.size * seq) % (vq.shape[1] * 16) == 0
        and 2 * (seq + 1) * aq.size <= vq.size
        and weight.size * 2 <= 10 * 2**20
        and vq.shape[0] <= 128
        and seq <= 8
    )


def solution(mesh):
    def step(*operands):
        if fits(mesh, operands):
            return fused(mesh.shape["seq"], mesh.shape["tensor"], *operands)
        return local(*operands)

    in_specs = (
        P(("groups", "seq"), "tensor"),
        P(("groups", "seq"), "tensor"),
        P(("groups", "seq"), "tensor"),
        P(("groups", "seq"), "tensor"),
        P("tensor", None),
        P(("groups", "seq"), "tensor"),
        P(("groups", "seq"), "tensor"),
        P(("groups", "seq"), "tensor"),
        P(("groups", "seq"), "tensor"),
        P(("groups", "seq"), "tensor"),
        P(("groups", "seq"), "tensor"),
    )
    out_specs = (
        P(("groups", "seq"), "tensor"),
        P(("groups", "seq"), "tensor"),
        P(("groups", "seq"), "tensor"),
    )
    return jax.shard_map(step, mesh=mesh, in_specs=in_specs, out_specs=out_specs, check_vma=False)
```

```python
import functools
import math

import jax
import jax.numpy as jnp
from jax import lax
from jax.experimental import pallas as pl
from jax.experimental.pallas import tpu as pltpu
from jax.sharding import PartitionSpec as P

HD = 128


def blank_state(query_rows, head_count):
    return (
        jnp.full((head_count, query_rows), -1e30, jnp.float32),
        jnp.zeros((head_count, query_rows), jnp.float32),
        jnp.zeros((head_count, query_rows, HD), jnp.float32),
    )


def absorb(carried, queries, keyset, values, head_count):
    running, row_sum, numerator = carried
    query_rows = queries.shape[0]
    key_rows = keyset.shape[0]
    factor = 1.0 / math.sqrt(HD)
    query_heads = queries.reshape(query_rows, head_count, HD)
    for offset in range(0, key_rows, 1024):
        width_keys = min(1024, key_rows - offset)
        key_block = keyset[offset : offset + width_keys].reshape(width_keys, head_count, HD)
        value_block = values[offset : offset + width_keys].reshape(width_keys, head_count, HD)
        scores = (
            jnp.einsum("qhd,khd->hqk", query_heads, key_block, preferred_element_type=jnp.float32)
            * factor
        )
        highest = jnp.maximum(running, jnp.max(scores, axis=2))
        raised = jnp.exp(scores - highest[:, :, None])
        shrink = jnp.exp(running - highest)
        row_sum = row_sum * shrink + jnp.sum(raised, axis=2)
        numerator = numerator * shrink[:, :, None] + jnp.einsum(
            "hqk,khd->hqd",
            raised.astype(jnp.bfloat16),
            value_block,
            preferred_element_type=jnp.float32,
        )
        running = highest
    return (running, row_sum, numerator)


def finish(carried, head_count):
    running, row_sum, numerator = carried
    result = numerator / row_sum[:, :, None]
    return result.transpose(1, 0, 2).reshape(result.shape[1], head_count * HD).astype(jnp.bfloat16)


def local(
    video_query,
    video_key,
    video_value,
    video_stream,
    out_weight,
    cross_query,
    audio_key,
    audio_value,
    audio_query,
    cross_key,
    cross_value,
):
    local_heads = video_query.shape[1] // HD
    query_rows = video_query.shape[0]
    pieces = (
        lax.all_gather(video_key, "seq", axis=0, tiled=True),
        lax.all_gather(video_value, "seq", axis=0, tiled=True),
    )
    carried_video = absorb(
        blank_state(query_rows, local_heads), video_query, pieces[0], pieces[1], local_heads
    )
    attended = finish(carried_video, local_heads)
    projected = jnp.dot(attended, out_weight, preferred_element_type=jnp.float32)
    summed = lax.psum_scatter(
        projected.astype(jnp.bfloat16), "tensor", scatter_dimension=1, tiled=True
    ).astype(jnp.float32)
    video_next = (video_stream.astype(jnp.float32) + summed).astype(jnp.bfloat16)
    cross_heads = cross_query.shape[1] // HD
    every_key, every_value = (
        lax.all_gather(audio_key, "seq", axis=0, tiled=True),
        lax.all_gather(audio_value, "seq", axis=0, tiled=True),
    )
    carried_audio = absorb(
        blank_state(cross_query.shape[0], cross_heads),
        cross_query,
        every_key,
        every_value,
        cross_heads,
    )
    video_cross = finish(carried_audio, cross_heads)
    pieces = (
        lax.all_gather(cross_key, "seq", axis=0, tiled=True),
        lax.all_gather(cross_value, "seq", axis=0, tiled=True),
    )
    carried_cross = absorb(
        blank_state(audio_query.shape[0], cross_heads),
        audio_query,
        pieces[0],
        pieces[1],
        cross_heads,
    )
    audio_cross = finish(carried_cross, cross_heads)
    return (video_next, video_cross, audio_cross)


MESH = pl.DeviceIdType.MESH
NT = (((1,), (1,)), ((), ()))
WIDE = 512
SHARES = (4, 3, 1)
SPLIT = True


def softmax_parts(queries, keyset, values):
    scores = lax.dot_general(queries, keyset, NT, preferred_element_type=jnp.float32) * (
        1.0 / math.sqrt(HD)
    )
    highest = jnp.max(scores, axis=1, keepdims=True)
    raised = jnp.exp(scores - highest)
    row_sum = jnp.sum(raised, axis=1, keepdims=True)
    numerator = jnp.dot(raised.astype(jnp.bfloat16), values, preferred_element_type=jnp.float32)
    return highest, row_sum, numerator


def row_cuts(rows):
    tiles, whole = rows // 16, sum(SHARES)
    marks = sorted({tiles * sum(SHARES[: i + 1]) // whole for i in range(len(SHARES))} | {0})
    return [(16 * a, 16 * (b - a)) for a, b in zip(marks, marks[1:])]


def by_distance(me, seq):
    right = (me < seq - 1 - me).astype(jnp.int32)
    toward = 2 * right - 1
    short = right * me + (1 - right) * (seq - 1 - me)
    order = []
    for i in range(seq - 1):
        both = (i < 2 * short).astype(jnp.int32)
        near = (i // 2 + 1) * (1 if i % 2 == 0 else -1)
        order.append(me + toward * (both * near + (1 - both) * (i - short + 1)))
    return order


def block_kernel(
    seq,
    tensor,
    vq,
    vk,
    vv,
    vs,
    weight,
    cq,
    ak,
    av,
    aq,
    ck,
    cv,
    next_ref,
    vcross_ref,
    across_ref,
    kv,
    q_all,
    heads_out,
    gathered,
    audio,
    partial,
    partial_in,
    cross_v,
    stream_v,
    weight_v,
    kept,
    mine,
    other,
    pair_out,
    pair_in,
    far_out,
    far_in,
    token,
    beside,
    kv_send,
    kv_recv,
    q_send,
    q_recv,
    own_sem,
    out_send,
    out_recv,
    out_last,
    audio_send,
    audio_recv,
    audio_own,
    part_send,
    part_recv,
    cross_sem,
    stream_sem,
    weight_sem,
    pair_send,
    pair_recv,
    home_recv,
    far_send,
    far_recv,
):
    rows = vq.shape[0]
    span = vq.shape[1] // seq
    share = span // HD
    cross_heads = cq.shape[1] // HD
    audio_rows, cross_width = aq.shape
    chips = tensor // 2
    width = next_ref.shape[1]
    pieces = width // WIDE
    cuts = row_cuts(rows)
    groups = len(cuts)
    me = lax.axis_index("seq")
    place = lax.axis_index("tensor")
    core = lax.rem(place, 2)
    chip = place // 2
    sibling = chip * 2 + (1 - core)
    peers = by_distance(me, seq)
    far_chips = [lax.rem(chip + d, chips) for d in range(chips)]

    def rows_of(p):
        return pl.ds(pl.multiple_of(p * rows, rows), rows)

    def audio_rows_of(p):
        return pl.ds(pl.multiple_of(p * audio_rows, audio_rows), audio_rows)

    def cols_of(p):
        return pl.ds(pl.multiple_of(p * span, span), span)

    def slot(p, r):
        start, size = cuts[r]
        return pl.ds(pl.multiple_of(seq * start + p * size, 16), size)

    for kind, ref in enumerate((vk, vv)):
        pltpu.make_async_copy(ref.at[:, cols_of(me)], kv.at[kind, rows_of(me)], own_sem).start()
    for r in range(groups):
        pltpu.make_async_copy(vq.at[pl.ds(*cuts[r]), cols_of(me)], q_all.at[slot(me, r)], own_sem).start()
    for kind, ref in enumerate((ak, av, aq)):
        pltpu.make_async_copy(ref, audio.at[kind, audio_rows_of(me)], audio_own).start()
    for kind, ref in enumerate((cq, ck, cv)):
        pltpu.make_async_copy(ref, cross_v.at[kind], cross_sem).start()
    stream_copy = pltpu.make_async_copy(vs, stream_v, stream_sem)
    stream_copy.start()

    def local_done(ref, sem):
        pltpu.make_async_copy(ref, ref, sem).wait()

    barrier = pltpu.get_barrier_semaphore()
    for way in (1, -1):

        @pl.when((me + way >= 0) & (me + way < seq))
        def _():
            pl.semaphore_signal(barrier, inc=1, device_id={"seq": me + way}, device_id_type=MESH)

    pl.semaphore_signal(barrier, inc=1, device_id={"tensor": sibling}, device_id_type=MESH)
    for d in range(1, chips):
        pl.semaphore_signal(
            barrier, inc=1, device_id={"tensor": far_chips[d] * 2 + core}, device_id_type=MESH
        )
    inner = ((me > 0) & (me < seq - 1)).astype(jnp.int32)
    with jax.named_scope("barrier"):
        pl.semaphore_wait(barrier, chips + 1 + inner)

    def to_seq(src, dst, send_sem, recv_sem, p):
        return pltpu.make_async_remote_copy(
            src_ref=src,
            dst_ref=dst,
            send_sem=send_sem,
            recv_sem=recv_sem,
            device_id={"seq": p},
            device_id_type=MESH,
        )

    def all_of(ref, send_sem, recv_sem):
        return to_seq(ref, ref, send_sem, recv_sem, peers[0])

    def keys_to(p, kinds=(0, 1)):
        for kind, ref in zip(kinds, (vk, vv)[kinds[0] :]):
            to_seq(ref.at[:, cols_of(p)], kv.at[kind, rows_of(me)], kv_send, kv_recv, p).start()

    def send_queries(r):
        here = pl.ds(*cuts[r])
        for p in peers[::-1]:
            to_seq(vq.at[here, cols_of(p)], q_all.at[slot(me, r)], q_send, q_recv.at[r], p).start()

    def audio_hop(step, way, part):
        shard = lax.rem(me - way * step + seq, seq)
        here = audio_rows_of(shard)
        block = audio.at[2, here] if part else audio.at[pl.ds(0, 2), here]
        return to_seq(
            block,
            block,
            audio_send.at[part],
            audio_recv.at[part, shard],
            lax.rem(me + way + seq, seq),
        )

    def on_line(step, way):
        source, target = me - way * step, me + way
        return (source >= 0) & (source < seq) & (target >= 0) & (target < seq)

    def pass_audio(step, part):
        for way in (1, -1):

            @pl.when(on_line(step, way))
            def _():
                copy = audio_hop(step, way, part)
                if step:
                    copy.wait_recv()
                copy.start()

    def crosses(way):
        return me == (seq // 2 - 1 if way > 0 else seq // 2)

    def some_audio(steps, chosen):
        for step in steps:
            for way in (1, -1):

                @pl.when(on_line(step, way) & chosen(step, way))
                def _():
                    copy = audio_hop(step, way, 0)
                    if step:
                        copy.wait_recv()
                    copy.start()

    def early_part():
        some_audio((0,), lambda step, way: jnp.logical_not(crosses(way)))

    def cross_part():
        some_audio((0, 1), lambda step, way: crosses(way))

    def relay_part():
        some_audio(range(1, seq - 1), lambda step, way: (step > 1) | jnp.logical_not(crosses(way)))

    def end_audio(part):
        for step in range(1, seq):
            for way in (1, -1):
                source, target = me - way * step, me + way
                last = (target < 0) | (target >= seq)

                @pl.when((source >= 0) & (source < seq) & last)
                def _():
                    audio_hop(step, way, part).wait_recv()

    def token_to(way):
        pl.semaphore_signal(
            token.at[(way + 1) // 2], inc=1, device_id={"seq": me + way}, device_id_type=MESH
        )

    def within(p):
        return (p >= 0) & (p < seq)

    def first_tokens():
        for way in (1, -1):

            @pl.when(within(me - way) & jnp.logical_not(within(me - 2 * way)) & within(me + way))
            def _():
                token_to(way)

    def tokens():
        for way in (1, -1):

            @pl.when(within(me - 2 * way))
            def _():
                pl.semaphore_wait(token.at[(way + 1) // 2], 1)

            @pl.when(within(me - 2 * way) & within(me + way))
            def _():
                token_to(way)

    local_done(audio.at[:, audio_rows_of(0)], audio_own)
    def run(name, f, *args):
        with jax.named_scope(name):
            f(*args)

    def late_audio(part):
        for step in range(2, seq - 1):
            pass_audio(step, part)

    def meet():
        pl.semaphore_signal(
            beside.at[0], inc=1, device_id={"tensor": sibling}, device_id_type=MESH
        )
        pl.semaphore_wait(beside.at[0], 1)

    run("p0", pass_audio, 0, 1)
    run("K0", keys_to, peers[0])
    run("tk1", first_tokens)
    run("tok", tokens)
    run("sib", meet)
    run("K1", keys_to, peers[1])
    run("K2", keys_to, peers[2])
    run("q0", send_queries, 0)
    run("PE", early_part)
    run("p1", pass_audio, 1, 1)
    weight_copy = pltpu.make_async_copy(weight, weight_v, weight_sem)
    weight_copy.start()

    def wait_keys():
        local_done(kv.at[:, pl.ds(0, rows * 3 // 2)], own_sem)
        all_of(kv.at[:, pl.ds(0, (seq - 1) * rows)], kv_send, kv_recv).wait_recv()

    def attend_rows(r):
        start, size = cuts[r]
        all_of(q_all.at[pl.ds(0, (seq - 1) * size)], q_send, q_recv.at[r]).wait_recv()
        block = pl.ds(seq * start, seq * size)
        for h in range(share):
            cols = slice(h * HD, (h + 1) * HD)
            _, row_sum, numerator = softmax_parts(q_all[block, cols], kv[0, :, cols], kv[1, :, cols])
            heads_out[block, cols] = (numerator / row_sum).astype(jnp.bfloat16)
        here = pl.ds(start, size)
        for p in peers[::-1]:
            sem = out_last.at[me] if SPLIT and r == groups - 1 else out_recv.at[r]
            to_seq(heads_out.at[slot(p, r)], gathered.at[me, here], out_send, sem, p).start()
        gathered[me, here] = heads_out[slot(me, r)]

    def upper(value):
        return value.astype(jnp.bfloat16).astype(jnp.float32)

    def cross_audio():
        local_done(cross_v, cross_sem)
        end_audio(1)
        lane = lax.broadcasted_iota(jnp.int32, (seq * audio_rows, HD), 1)
        held = jnp.zeros((seq * audio_rows, HD), jnp.float32)
        for c in range(cross_heads):
            cols = slice(c * HD, (c + 1) * HD)
            highest, row_sum, numerator = softmax_parts(
                audio[2, :, cols], cross_v[1, :, cols], cross_v[2, :, cols]
            )
            for i, value in enumerate((highest, row_sum)):
                held = jnp.where(lane == 2 * (2 * c + i), upper(value), held)
                held = jnp.where(lane == 2 * (2 * c + i) + 1, value - upper(value), held)
            partial[:, cols] = numerator.astype(jnp.bfloat16)
        partial[:, cross_heads * HD :] = held.astype(jnp.bfloat16)

    def cross_video():
        end_audio(0)
        for c in range(cross_heads):
            cols = slice(c * HD, (c + 1) * HD)
            _, row_sum, numerator = softmax_parts(
                cross_v[0, :, cols], audio[0, :, cols], audio[1, :, cols]
            )
            vcross_ref[:, cols] = (numerator / row_sum).astype(jnp.bfloat16)

    def cross_send():
        for p in peers:
            theirs = audio_rows_of(p)
            to_seq(partial.at[theirs], partial_in.at[me], part_send, part_recv, p).start()

    def cross_finish():
        all_of(partial_in.at[pl.ds(0, seq - 1)], part_send, part_recv).wait_recv()
        my_audio = audio_rows_of(me)
        stat_cols = slice(cross_heads * HD, (cross_heads + 1) * HD)
        held = [partial[my_audio, stat_cols]] + [partial_in[p, :, stat_cols] for p in peers]
        held = [value.astype(jnp.float32) for value in held]

        def stat(s, i):
            return s[:, 2 * i : 2 * i + 1] + s[:, 2 * i + 1 : 2 * i + 2]

        for c in range(cross_heads):
            cols = slice(c * HD, (c + 1) * HD)
            parts = [partial[my_audio, cols]] + [partial_in[p, :, cols] for p in peers]
            tops = [stat(s, 2 * c) for s in held]
            sums = [stat(s, 2 * c + 1) for s in held]
            highest = functools.reduce(jnp.maximum, tops)
            factors = [jnp.exp(t - highest) for t in tops]
            row_sum = sum(f * s for f, s in zip(factors, sums))
            numerator = sum(f * n.astype(jnp.float32) for f, n in zip(factors, parts))
            across_ref[:, cols] = (numerator / row_sum).astype(jnp.bfloat16)

    def product(attended, d, side, j):
        target = far_chips[d] * 2 + (core if side else 1 - core)
        cols = pl.ds(pl.multiple_of(target * width + j * WIDE, WIDE), WIDE)
        return jnp.dot(attended, weight_v[:, cols], preferred_element_type=jnp.float32)

    def pair_copy(r, d):
        here = pl.ds(*cuts[r])
        return pltpu.make_async_remote_copy(
            src_ref=pair_out.at[d, here],
            dst_ref=pair_in.at[d, here],
            send_sem=pair_send,
            recv_sem=pair_recv.at[r, d - 1],
            device_id={"tensor": sibling},
            device_id_type=MESH,
        )

    def far_copy(r, d):
        here = pl.ds(*cuts[r])
        return pltpu.make_async_remote_copy(
            src_ref=far_out.at[d - 1, here],
            dst_ref=far_in.at[d - 1, here],
            send_sem=far_send,
            recv_sem=far_recv.at[r, d - 1],
            device_id={"tensor": far_chips[d] * 2 + core},
            device_id_type=MESH,
        )

    home_copy = pltpu.make_async_remote_copy(
        src_ref=pair_out.at[0],
        dst_ref=pair_in.at[0],
        send_sem=pair_send,
        recv_sem=home_recv,
        device_id={"tensor": sibling},
        device_id_type=MESH,
    )
    blocks = [slice(j * WIDE, (j + 1) * WIDE) for j in range(pieces)]

    def share_rows(r):
        here = pl.ds(*cuts[r])
        all_of(gathered.at[pl.ds(0, seq - 1), here], out_send, out_recv.at[r]).wait_recv()
        attended = jnp.concatenate([gathered[p, here] for p in range(seq)], axis=1)
        if r == 0:
            weight_copy.wait()
        for d in range(1, chips):
            for j, block in enumerate(blocks):
                pair_out[d, here, block] = product(attended, d, 0, j).astype(jnp.bfloat16)
            pair_copy(r, d).start()
        for d in range(1, chips):
            for j, block in enumerate(blocks):
                mine[d - 1, here, block] = product(attended, d, 1, j)

    def share_parts(r):
        here = pl.ds(*cuts[r])

        def add_part(some, d, side, first):
            target = far_chips[d] * 2 + (core if side else 1 - core)
            for j, block in enumerate(blocks):
                cols = pl.ds(pl.multiple_of(target * width + j * WIDE, WIDE), WIDE)
                value = sum(
                    jnp.dot(gathered[p, here], weight_v[cols_of(p), cols], preferred_element_type=jnp.float32)
                    for p in some
                )
                ref = mine if side else other
                ref[d - 1, here, block] = value if first else ref[d - 1, here, block] + value

        some = [me]
        for i, p in enumerate(peers):
            all_of(gathered.at[0, here], out_send, out_last.at[p]).wait_recv()
            some.append(p)
            if i == 0 and len(peers) > 1:
                continue
            for side in (0, 1):
                for d in range(1, chips):
                    add_part(some, d, side, i <= 1)
                    if side == 0 and i == len(peers) - 1:
                        pair_out[d, here] = other[d - 1, here].astype(jnp.bfloat16)
                        pair_copy(r, d).start()
            some = []

    def send_far(r):
        here = pl.ds(*cuts[r])
        for d in range(1, chips):
            pair_copy(r, d).wait_recv()
            far_out[d - 1, here] = (mine[d - 1, here] + pair_in[d, here].astype(jnp.float32)).astype(
                jnp.bfloat16
            )
            far_copy(r, d).start()

    def all_heads():
        return jnp.concatenate([gathered[p] for p in range(seq)], axis=1)

    def give_home():
        attended = all_heads()
        for j, block in enumerate(blocks):
            pair_out[0, :, block] = product(attended, 0, 0, j).astype(jnp.bfloat16)
        home_copy.start()

    def keep_home():
        attended = all_heads()
        stream_copy.wait()
        for j, block in enumerate(blocks):
            kept[:, block] = product(attended, 0, 1, j) + stream_v[:, block].astype(jnp.float32)

    def close_rows(r):
        here = pl.ds(*cuts[r])
        value = kept[here] + pair_in[0, here].astype(jnp.float32)
        for d in range(1, chips):
            far_copy(r, d).wait_recv()
            value = value + far_in[d - 1, here].astype(jnp.float32)
        next_ref[here] = value.astype(jnp.bfloat16)

    def settle():
        all_of(kv.at[:, pl.ds(0, (seq - 1) * rows)], kv_send, kv_recv).wait_send()
        all_of(q_all.at[pl.ds(0, (seq - 1) * rows)], q_send, q_recv.at[0]).wait_send()
        all_of(heads_out.at[pl.ds(0, (seq - 1) * rows)], out_send, out_recv.at[0]).wait_send()
        all_of(partial.at[pl.ds(0, (seq - 1) * audio_rows)], part_send, part_recv).wait_send()
        block = audio_rows * cross_width // span
        for part, count in ((0, 2), (1, 1)):
            for hops, place_fits in ((1, inner == 0), (seq + 1, inner == 1)):

                @pl.when(place_fits)
                def _():
                    some = heads_out.at[pl.ds(0, hops * count * block)]
                    all_of(some, audio_send.at[part], audio_recv.at[part, 0]).wait_send()

        all_of(pair_out, pair_send, pair_recv.at[0, 0]).wait_send()
        if chips > 1:
            all_of(far_out, far_send, far_recv.at[0, 0]).wait_send()

    run("wk", wait_keys)
    run("q1", send_queries, 1)
    run("p2", late_audio, 1)
    run("a0", attend_rows, 0)
    run("q2", send_queries, 2)
    run("a1", attend_rows, 1)
    run("ca", cross_audio)
    run("A0", share_rows, 0)
    run("PL", cross_part)
    @pl.when(core == 0)
    def _():
        run("B0", send_far, 0)

    run("a2", attend_rows, 2)
    @pl.when(core == 1)
    def _():
        run("B0", send_far, 0)

    @pl.when(core == 1)
    def _():
        run("PR", relay_part)

    run("A1", share_rows, 1)
    run("B1", send_far, 1)
    @pl.when(core == 0)
    def _():
        run("PR", relay_part)

    run("cs", cross_send)
    run("A2", share_parts, 2)
    @pl.when(core == 1)
    def _():
        run("k0", give_home)

    @pl.when(core == 1)
    def _():
        run("k1", keep_home)

    run("B2", send_far, 2)
    @pl.when(core == 0)
    def _():
        run("k0", give_home)

    @pl.when(core == 0)
    def _():
        run("k1", keep_home)

    run("cf", cross_finish)
    run("cv", cross_video)
    run("h", home_copy.wait_recv)
    run("c0", close_rows, 0)
    run("c1", close_rows, 1)
    run("c2", close_rows, 2)
    with jax.named_scope("settle"):
        settle()


def write_out(*refs):
    half = len(refs) // 2
    for src, dst in zip(refs[:half], refs[half:]):
        dst[...] = src[...]


def fused(seq, tensor, *operands):
    vq, vk, vv, vs, weight, cq, ak, av, aq, ck, cv = operands
    rows, features = vq.shape
    span = features // seq
    audio_rows, cross_width = aq.shape
    chips = tensor // 2
    width = weight.shape[1] // tensor
    groups = len(row_cuts(rows))
    others = max(chips - 1, 1)
    bf16, f32, dma = jnp.bfloat16, jnp.float32, pltpu.SemaphoreType.DMA
    shapes = tuple(jax.ShapeDtypeStruct(x.shape, bf16) for x in (vs, cq, aq))
    whole = pl.BlockSpec(memory_space=pltpu.VMEM)
    results = pl.pallas_call(
        functools.partial(block_kernel, seq, tensor),
        out_shape=tuple(pltpu.VMEM(x.shape, bf16) for x in (vs, cq, aq)),
        in_specs=[pl.BlockSpec(memory_space=pltpu.HBM)] * 11,
        out_specs=(whole,) * 3,
        scratch_shapes=[
            pltpu.VMEM((2, seq * rows, span), bf16),
            pltpu.VMEM((seq * rows, span), bf16),
            pltpu.VMEM((seq * rows, span), bf16),
            pltpu.VMEM((seq, rows, span), bf16),
            pltpu.VMEM((3, seq * audio_rows, cross_width), bf16),
            pltpu.VMEM((seq * audio_rows, cross_width + HD), bf16),
            pltpu.VMEM((seq, audio_rows, cross_width + HD), bf16),
            pltpu.VMEM((3, *cq.shape), bf16),
            pltpu.VMEM(vs.shape, bf16),
            pltpu.VMEM(weight.shape, bf16),
            pltpu.VMEM(vs.shape, f32),
            pltpu.VMEM((others, rows, width), f32),
            pltpu.VMEM((others, rows, width), f32),
            pltpu.VMEM((chips, rows, width), bf16),
            pltpu.VMEM((chips, rows, width), bf16),
            pltpu.VMEM((others, rows, width), bf16),
            pltpu.VMEM((others, rows, width), bf16),
            pltpu.SemaphoreType.REGULAR((2,)),
            pltpu.SemaphoreType.REGULAR((1,)),
            dma(()),
            dma(()),
            dma(()),
            dma((groups,)),
            dma(()),
            dma(()),
            dma((groups,)),
            dma((seq,)),
            dma((2,)),
            dma((2, seq)),
            dma(()),
            dma(()),
            dma(()),
            dma(()),
            dma(()),
            dma(()),
            dma(()),
            dma((groups, others)),
            dma(()),
            dma(()),
            dma((groups, others)),
        ],
        compiler_params=pltpu.CompilerParams(
            collective_id=0, has_side_effects=True, vmem_limit_bytes=60000000
        ),
    )(*operands)
    return pl.pallas_call(
        write_out,
        out_shape=shapes,
        in_specs=[whole] * 3,
        out_specs=(whole,) * 3,
        compiler_params=pltpu.CompilerParams(vmem_limit_bytes=8 * 2**20),
    )(*results)


def fits(mesh, operands):
    seq, tensor = mesh.shape["seq"], mesh.shape["tensor"]
    vq, weight, cq, aq = operands[0], operands[4], operands[5], operands[8]
    return (
        seq > 1
        and (vq.shape[1] // HD) % seq == 0
        and tensor % 2 == 0
        and (weight.shape[1] // tensor) % WIDE == 0
        and aq.shape[0] % 16 == 0
        and vq.shape[0] % 16 == 0
        and 4 * (cq.shape[1] // HD) <= HD
        and (aq.size * seq) % (vq.shape[1] * 16) == 0
        and 2 * (seq + 1) * aq.size <= vq.size
        and weight.size * 2 <= 10 * 2**20
        and vq.shape[0] <= 128
        and seq <= 8
    )


def solution(mesh):
    def step(*operands):
        if fits(mesh, operands):
            return fused(mesh.shape["seq"], mesh.shape["tensor"], *operands)
        return local(*operands)

    in_specs = (
        P(("groups", "seq"), "tensor"),
        P(("groups", "seq"), "tensor"),
        P(("groups", "seq"), "tensor"),
        P(("groups", "seq"), "tensor"),
        P("tensor", None),
        P(("groups", "seq"), "tensor"),
        P(("groups", "seq"), "tensor"),
        P(("groups", "seq"), "tensor"),
        P(("groups", "seq"), "tensor"),
        P(("groups", "seq"), "tensor"),
        P(("groups", "seq"), "tensor"),
    )
    out_specs = (
        P(("groups", "seq"), "tensor"),
        P(("groups", "seq"), "tensor"),
        P(("groups", "seq"), "tensor"),
    )
    return jax.shard_map(step, mesh=mesh, in_specs=in_specs, out_specs=out_specs, check_vma=False)
```

```python
import functools
import math

import jax
import jax.numpy as jnp
from jax import lax
from jax.experimental import pallas as pl
from jax.experimental.pallas import tpu as pltpu
from jax.sharding import PartitionSpec as P

HD = 128


def blank_state(query_rows, head_count):
    return (
        jnp.full((head_count, query_rows), -1e30, jnp.float32),
        jnp.zeros((head_count, query_rows), jnp.float32),
        jnp.zeros((head_count, query_rows, HD), jnp.float32),
    )


def absorb(carried, queries, keyset, values, head_count):
    running, row_sum, numerator = carried
    query_rows = queries.shape[0]
    key_rows = keyset.shape[0]
    factor = 1.0 / math.sqrt(HD)
    query_heads = queries.reshape(query_rows, head_count, HD)
    for offset in range(0, key_rows, 1024):
        width_keys = min(1024, key_rows - offset)
        key_block = keyset[offset : offset + width_keys].reshape(width_keys, head_count, HD)
        value_block = values[offset : offset + width_keys].reshape(width_keys, head_count, HD)
        scores = (
            jnp.einsum("qhd,khd->hqk", query_heads, key_block, preferred_element_type=jnp.float32)
            * factor
        )
        highest = jnp.maximum(running, jnp.max(scores, axis=2))
        raised = jnp.exp(scores - highest[:, :, None])
        shrink = jnp.exp(running - highest)
        row_sum = row_sum * shrink + jnp.sum(raised, axis=2)
        numerator = numerator * shrink[:, :, None] + jnp.einsum(
            "hqk,khd->hqd",
            raised.astype(jnp.bfloat16),
            value_block,
            preferred_element_type=jnp.float32,
        )
        running = highest
    return (running, row_sum, numerator)


def finish(carried, head_count):
    running, row_sum, numerator = carried
    result = numerator / row_sum[:, :, None]
    return result.transpose(1, 0, 2).reshape(result.shape[1], head_count * HD).astype(jnp.bfloat16)


def local(
    video_query,
    video_key,
    video_value,
    video_stream,
    out_weight,
    cross_query,
    audio_key,
    audio_value,
    audio_query,
    cross_key,
    cross_value,
):
    local_heads = video_query.shape[1] // HD
    query_rows = video_query.shape[0]
    pieces = (
        lax.all_gather(video_key, "seq", axis=0, tiled=True),
        lax.all_gather(video_value, "seq", axis=0, tiled=True),
    )
    carried_video = absorb(
        blank_state(query_rows, local_heads), video_query, pieces[0], pieces[1], local_heads
    )
    attended = finish(carried_video, local_heads)
    projected = jnp.dot(attended, out_weight, preferred_element_type=jnp.float32)
    summed = lax.psum_scatter(
        projected.astype(jnp.bfloat16), "tensor", scatter_dimension=1, tiled=True
    ).astype(jnp.float32)
    video_next = (video_stream.astype(jnp.float32) + summed).astype(jnp.bfloat16)
    cross_heads = cross_query.shape[1] // HD
    every_key, every_value = (
        lax.all_gather(audio_key, "seq", axis=0, tiled=True),
        lax.all_gather(audio_value, "seq", axis=0, tiled=True),
    )
    carried_audio = absorb(
        blank_state(cross_query.shape[0], cross_heads),
        cross_query,
        every_key,
        every_value,
        cross_heads,
    )
    video_cross = finish(carried_audio, cross_heads)
    pieces = (
        lax.all_gather(cross_key, "seq", axis=0, tiled=True),
        lax.all_gather(cross_value, "seq", axis=0, tiled=True),
    )
    carried_cross = absorb(
        blank_state(audio_query.shape[0], cross_heads),
        audio_query,
        pieces[0],
        pieces[1],
        cross_heads,
    )
    audio_cross = finish(carried_cross, cross_heads)
    return (video_next, video_cross, audio_cross)


MESH = pl.DeviceIdType.MESH
NT = (((1,), (1,)), ((), ()))
WIDE = 512
SHARES = (4, 3, 1)
SPLIT = True


def softmax_parts(queries, keyset, values):
    scores = lax.dot_general(queries, keyset, NT, preferred_element_type=jnp.float32) * (
        1.0 / math.sqrt(HD)
    )
    highest = jnp.max(scores, axis=1, keepdims=True)
    raised = jnp.exp(scores - highest)
    row_sum = jnp.sum(raised, axis=1, keepdims=True)
    numerator = jnp.dot(raised.astype(jnp.bfloat16), values, preferred_element_type=jnp.float32)
    return highest, row_sum, numerator


def row_cuts(rows):
    tiles, whole = rows // 16, sum(SHARES)
    marks = sorted({tiles * sum(SHARES[: i + 1]) // whole for i in range(len(SHARES))} | {0})
    return [(16 * a, 16 * (b - a)) for a, b in zip(marks, marks[1:])]


def by_distance(me, seq):
    right = (me < seq - 1 - me).astype(jnp.int32)
    toward = 2 * right - 1
    short = right * me + (1 - right) * (seq - 1 - me)
    order = []
    for i in range(seq - 1):
        both = (i < 2 * short).astype(jnp.int32)
        near = (i // 2 + 1) * (1 if i % 2 == 0 else -1)
        order.append(me + toward * (both * near + (1 - both) * (i - short + 1)))
    return order


def block_kernel(
    seq,
    tensor,
    vq,
    vk,
    vv,
    vs,
    weight,
    cq,
    ak,
    av,
    aq,
    ck,
    cv,
    next_ref,
    vcross_ref,
    across_ref,
    kv,
    q_all,
    heads_out,
    gathered,
    audio,
    partial,
    partial_in,
    cross_v,
    stream_v,
    weight_v,
    kept,
    mine,
    other,
    pair_out,
    pair_in,
    far_out,
    far_in,
    token,
    beside,
    kv_send,
    kv_recv,
    q_send,
    q_recv,
    own_sem,
    out_send,
    out_recv,
    out_last,
    audio_send,
    audio_recv,
    audio_own,
    part_send,
    part_recv,
    cross_sem,
    stream_sem,
    weight_sem,
    pair_send,
    pair_recv,
    home_recv,
    far_send,
    far_recv,
):
    rows = vq.shape[0]
    span = vq.shape[1] // seq
    share = span // HD
    cross_heads = cq.shape[1] // HD
    audio_rows, cross_width = aq.shape
    chips = tensor // 2
    width = next_ref.shape[1]
    pieces = width // WIDE
    cuts = row_cuts(rows)
    groups = len(cuts)
    me = lax.axis_index("seq")
    place = lax.axis_index("tensor")
    core = lax.rem(place, 2)
    chip = place // 2
    sibling = chip * 2 + (1 - core)
    peers = by_distance(me, seq)
    far_chips = [lax.rem(chip + d, chips) for d in range(chips)]

    def rows_of(p):
        return pl.ds(pl.multiple_of(p * rows, rows), rows)

    def audio_rows_of(p):
        return pl.ds(pl.multiple_of(p * audio_rows, audio_rows), audio_rows)

    def cols_of(p):
        return pl.ds(pl.multiple_of(p * span, span), span)

    def slot(p, r):
        start, size = cuts[r]
        return pl.ds(pl.multiple_of(seq * start + p * size, 16), size)

    for kind, ref in enumerate((vk, vv)):
        pltpu.make_async_copy(ref.at[:, cols_of(me)], kv.at[kind, rows_of(me)], own_sem).start()
    for r in range(groups):
        pltpu.make_async_copy(vq.at[pl.ds(*cuts[r]), cols_of(me)], q_all.at[slot(me, r)], own_sem).start()
    for kind, ref in enumerate((ak, av, aq)):
        pltpu.make_async_copy(ref, audio.at[kind, audio_rows_of(me)], audio_own).start()
    for kind, ref in enumerate((cq, ck, cv)):
        pltpu.make_async_copy(ref, cross_v.at[kind], cross_sem).start()
    stream_copy = pltpu.make_async_copy(vs, stream_v, stream_sem)
    stream_copy.start()

    def local_done(ref, sem):
        pltpu.make_async_copy(ref, ref, sem).wait()

    barrier = pltpu.get_barrier_semaphore()
    for way in (1, -1):

        @pl.when((me + way >= 0) & (me + way < seq))
        def _():
            pl.semaphore_signal(barrier, inc=1, device_id={"seq": me + way}, device_id_type=MESH)

    pl.semaphore_signal(barrier, inc=1, device_id={"tensor": sibling}, device_id_type=MESH)
    for d in range(1, chips):
        pl.semaphore_signal(
            barrier, inc=1, device_id={"tensor": far_chips[d] * 2 + core}, device_id_type=MESH
        )
    inner = ((me > 0) & (me < seq - 1)).astype(jnp.int32)
    with jax.named_scope("barrier"):
        pl.semaphore_wait(barrier, chips + 1 + inner)

    def to_seq(src, dst, send_sem, recv_sem, p):
        return pltpu.make_async_remote_copy(
            src_ref=src,
            dst_ref=dst,
            send_sem=send_sem,
            recv_sem=recv_sem,
            device_id={"seq": p},
            device_id_type=MESH,
        )

    def all_of(ref, send_sem, recv_sem):
        return to_seq(ref, ref, send_sem, recv_sem, peers[0])

    def keys_to(p, kinds=(0, 1)):
        for kind, ref in zip(kinds, (vk, vv)[kinds[0] :]):
            to_seq(ref.at[:, cols_of(p)], kv.at[kind, rows_of(me)], kv_send, kv_recv, p).start()

    def send_queries(r):
        here = pl.ds(*cuts[r])
        for p in peers[::-1]:
            to_seq(vq.at[here, cols_of(p)], q_all.at[slot(me, r)], q_send, q_recv.at[r], p).start()

    def audio_hop(step, way, part):
        shard = lax.rem(me - way * step + seq, seq)
        here = audio_rows_of(shard)
        block = audio.at[2, here] if part else audio.at[pl.ds(0, 2), here]
        return to_seq(
            block,
            block,
            audio_send.at[part],
            audio_recv.at[part, shard],
            lax.rem(me + way + seq, seq),
        )

    def on_line(step, way):
        source, target = me - way * step, me + way
        return (source >= 0) & (source < seq) & (target >= 0) & (target < seq)

    def pass_audio(step, part):
        for way in (1, -1):

            @pl.when(on_line(step, way))
            def _():
                copy = audio_hop(step, way, part)
                if step:
                    copy.wait_recv()
                copy.start()

    def crosses(way):
        return me == (seq // 2 - 1 if way > 0 else seq // 2)

    def some_audio(steps, chosen):
        for step in steps:
            for way in (1, -1):

                @pl.when(on_line(step, way) & chosen(step, way))
                def _():
                    copy = audio_hop(step, way, 0)
                    if step:
                        copy.wait_recv()
                    copy.start()

    def early_part():
        some_audio((0,), lambda step, way: jnp.logical_not(crosses(way)))

    def cross_part():
        some_audio((0, 1), lambda step, way: crosses(way))

    def relay_part():
        some_audio(range(1, seq - 1), lambda step, way: (step > 1) | jnp.logical_not(crosses(way)))

    def end_audio(part):
        for step in range(1, seq):
            for way in (1, -1):
                source, target = me - way * step, me + way
                last = (target < 0) | (target >= seq)

                @pl.when((source >= 0) & (source < seq) & last)
                def _():
                    audio_hop(step, way, part).wait_recv()

    def token_to(way):
        pl.semaphore_signal(
            token.at[(way + 1) // 2], inc=1, device_id={"seq": me + way}, device_id_type=MESH
        )

    def within(p):
        return (p >= 0) & (p < seq)

    def first_tokens():
        for way in (1, -1):

            @pl.when(within(me - way) & jnp.logical_not(within(me - 2 * way)) & within(me + way))
            def _():
                token_to(way)

    def tokens():
        for way in (1, -1):

            @pl.when(within(me - 2 * way))
            def _():
                pl.semaphore_wait(token.at[(way + 1) // 2], 1)

            @pl.when(within(me - 2 * way) & within(me + way))
            def _():
                token_to(way)

    local_done(audio.at[:, audio_rows_of(0)], audio_own)
    def run(name, f, *args):
        with jax.named_scope(name):
            f(*args)

    def late_audio(part):
        for step in range(2, seq - 1):
            pass_audio(step, part)

    def meet():
        pl.semaphore_signal(
            beside.at[0], inc=1, device_id={"tensor": sibling}, device_id_type=MESH
        )
        pl.semaphore_wait(beside.at[0], 1)

    run("p0", pass_audio, 0, 1)
    run("K0", keys_to, peers[0])
    run("tk1", first_tokens)
    run("tok", tokens)
    run("sib", meet)
    run("K1", keys_to, peers[1])
    run("K2", keys_to, peers[2])
    run("q0", send_queries, 0)
    run("PE", early_part)
    run("p1", pass_audio, 1, 1)
    weight_copy = pltpu.make_async_copy(weight, weight_v, weight_sem)
    weight_copy.start()

    def wait_keys():
        local_done(kv.at[:, pl.ds(0, rows * 3 // 2)], own_sem)
        all_of(kv.at[:, pl.ds(0, (seq - 1) * rows)], kv_send, kv_recv).wait_recv()

    def attend_rows(r):
        start, size = cuts[r]
        all_of(q_all.at[pl.ds(0, (seq - 1) * size)], q_send, q_recv.at[r]).wait_recv()
        block = pl.ds(seq * start, seq * size)
        for h in range(share):
            cols = slice(h * HD, (h + 1) * HD)
            _, row_sum, numerator = softmax_parts(q_all[block, cols], kv[0, :, cols], kv[1, :, cols])
            heads_out[block, cols] = (numerator / row_sum).astype(jnp.bfloat16)
        here = pl.ds(start, size)
        for p in peers[::-1]:
            sem = out_last.at[me] if SPLIT and r == groups - 1 else out_recv.at[r]
            to_seq(heads_out.at[slot(p, r)], gathered.at[me, here], out_send, sem, p).start()
        gathered[me, here] = heads_out[slot(me, r)]

    def upper(value):
        return value.astype(jnp.bfloat16).astype(jnp.float32)

    def cross_audio():
        local_done(cross_v, cross_sem)
        end_audio(1)
        lane = lax.broadcasted_iota(jnp.int32, (seq * audio_rows, HD), 1)
        held = jnp.zeros((seq * audio_rows, HD), jnp.float32)
        for c in range(cross_heads):
            cols = slice(c * HD, (c + 1) * HD)
            highest, row_sum, numerator = softmax_parts(
                audio[2, :, cols], cross_v[1, :, cols], cross_v[2, :, cols]
            )
            for i, value in enumerate((highest, row_sum)):
                for k in range(3):
                    piece = upper(value)
                    held = jnp.where(lane == 3 * (2 * c + i) + k, piece, held)
                    value = value - piece
            partial[:, cols] = numerator.astype(jnp.bfloat16)
        partial[:, cross_heads * HD :] = held.astype(jnp.bfloat16)

    def cross_video():
        end_audio(0)
        for c in range(cross_heads):
            cols = slice(c * HD, (c + 1) * HD)
            _, row_sum, numerator = softmax_parts(
                cross_v[0, :, cols], audio[0, :, cols], audio[1, :, cols]
            )
            vcross_ref[:, cols] = (numerator / row_sum).astype(jnp.bfloat16)

    def cross_send():
        for p in peers:
            theirs = audio_rows_of(p)
            to_seq(partial.at[theirs], partial_in.at[me], part_send, part_recv, p).start()

    def cross_finish():
        all_of(partial_in.at[pl.ds(0, seq - 1)], part_send, part_recv).wait_recv()
        my_audio = audio_rows_of(me)
        stat_cols = slice(cross_heads * HD, (cross_heads + 1) * HD)
        held = [partial[my_audio, stat_cols]] + [partial_in[p, :, stat_cols] for p in peers]
        held = [value.astype(jnp.float32) for value in held]

        def stat(s, i):
            return s[:, 3 * i : 3 * i + 1] + s[:, 3 * i + 1 : 3 * i + 2] + s[:, 3 * i + 2 : 3 * i + 3]

        for c in range(cross_heads):
            cols = slice(c * HD, (c + 1) * HD)
            parts = [partial[my_audio, cols]] + [partial_in[p, :, cols] for p in peers]
            tops = [stat(s, 2 * c) for s in held]
            sums = [stat(s, 2 * c + 1) for s in held]
            highest = functools.reduce(jnp.maximum, tops)
            factors = [jnp.exp(t - highest) for t in tops]
            row_sum = sum(f * s for f, s in zip(factors, sums))
            numerator = sum(f * n.astype(jnp.float32) for f, n in zip(factors, parts))
            across_ref[:, cols] = (numerator / row_sum).astype(jnp.bfloat16)

    def product(attended, d, side, j):
        target = far_chips[d] * 2 + (core if side else 1 - core)
        cols = pl.ds(pl.multiple_of(target * width + j * WIDE, WIDE), WIDE)
        return jnp.dot(attended, weight_v[:, cols], preferred_element_type=jnp.float32)

    def pair_copy(r, d):
        here = pl.ds(*cuts[r])
        return pltpu.make_async_remote_copy(
            src_ref=pair_out.at[d, here],
            dst_ref=pair_in.at[d, here],
            send_sem=pair_send,
            recv_sem=pair_recv.at[r, d - 1],
            device_id={"tensor": sibling},
            device_id_type=MESH,
        )

    def far_copy(r, d):
        here = pl.ds(*cuts[r])
        return pltpu.make_async_remote_copy(
            src_ref=far_out.at[d - 1, here],
            dst_ref=far_in.at[d - 1, here],
            send_sem=far_send,
            recv_sem=far_recv.at[r, d - 1],
            device_id={"tensor": far_chips[d] * 2 + core},
            device_id_type=MESH,
        )

    home_copy = pltpu.make_async_remote_copy(
        src_ref=pair_out.at[0],
        dst_ref=pair_in.at[0],
        send_sem=pair_send,
        recv_sem=home_recv,
        device_id={"tensor": sibling},
        device_id_type=MESH,
    )
    blocks = [slice(j * WIDE, (j + 1) * WIDE) for j in range(pieces)]

    def share_rows(r):
        here = pl.ds(*cuts[r])
        all_of(gathered.at[pl.ds(0, seq - 1), here], out_send, out_recv.at[r]).wait_recv()
        attended = jnp.concatenate([gathered[p, here] for p in range(seq)], axis=1)
        if r == 0:
            weight_copy.wait()
        for d in range(1, chips):
            for j, block in enumerate(blocks):
                pair_out[d, here, block] = product(attended, d, 0, j).astype(jnp.bfloat16)
            pair_copy(r, d).start()
        for d in range(1, chips):
            for j, block in enumerate(blocks):
                mine[d - 1, here, block] = product(attended, d, 1, j)

    def share_parts(r):
        here = pl.ds(*cuts[r])

        def add_part(some, d, side, first):
            target = far_chips[d] * 2 + (core if side else 1 - core)
            for j, block in enumerate(blocks):
                cols = pl.ds(pl.multiple_of(target * width + j * WIDE, WIDE), WIDE)
                value = sum(
                    jnp.dot(gathered[p, here], weight_v[cols_of(p), cols], preferred_element_type=jnp.float32)
                    for p in some
                )
                ref = mine if side else other
                ref[d - 1, here, block] = value if first else ref[d - 1, here, block] + value

        some = [me]
        for i, p in enumerate(peers):
            all_of(gathered.at[0, here], out_send, out_last.at[p]).wait_recv()
            some.append(p)
            if i == 0 and len(peers) > 1:
                continue
            for side in (0, 1):
                for d in range(1, chips):
                    add_part(some, d, side, i <= 1)
                    if side == 0 and i == len(peers) - 1:
                        pair_out[d, here] = other[d - 1, here].astype(jnp.bfloat16)
                        pair_copy(r, d).start()
            some = []

    def send_far(r):
        here = pl.ds(*cuts[r])
        for d in range(1, chips):
            pair_copy(r, d).wait_recv()
            far_out[d - 1, here] = (mine[d - 1, here] + pair_in[d, here].astype(jnp.float32)).astype(
                jnp.bfloat16
            )
            far_copy(r, d).start()

    def all_heads():
        return jnp.concatenate([gathered[p] for p in range(seq)], axis=1)

    def give_home():
        attended = all_heads()
        for j, block in enumerate(blocks):
            pair_out[0, :, block] = product(attended, 0, 0, j).astype(jnp.bfloat16)
        home_copy.start()

    def keep_home():
        attended = all_heads()
        stream_copy.wait()
        for j, block in enumerate(blocks):
            kept[:, block] = product(attended, 0, 1, j) + stream_v[:, block].astype(jnp.float32)

    def close_rows(r):
        here = pl.ds(*cuts[r])
        value = kept[here] + pair_in[0, here].astype(jnp.float32)
        for d in range(1, chips):
            far_copy(r, d).wait_recv()
            value = value + far_in[d - 1, here].astype(jnp.float32)
        next_ref[here] = value.astype(jnp.bfloat16)

    def settle():
        all_of(kv.at[:, pl.ds(0, (seq - 1) * rows)], kv_send, kv_recv).wait_send()
        all_of(q_all.at[pl.ds(0, (seq - 1) * rows)], q_send, q_recv.at[0]).wait_send()
        all_of(heads_out.at[pl.ds(0, (seq - 1) * rows)], out_send, out_recv.at[0]).wait_send()
        all_of(partial.at[pl.ds(0, (seq - 1) * audio_rows)], part_send, part_recv).wait_send()
        block = audio_rows * cross_width // span
        for part, count in ((0, 2), (1, 1)):
            for hops, place_fits in ((1, inner == 0), (seq + 1, inner == 1)):

                @pl.when(place_fits)
                def _():
                    some = heads_out.at[pl.ds(0, hops * count * block)]
                    all_of(some, audio_send.at[part], audio_recv.at[part, 0]).wait_send()

        all_of(pair_out, pair_send, pair_recv.at[0, 0]).wait_send()
        if chips > 1:
            all_of(far_out, far_send, far_recv.at[0, 0]).wait_send()

    run("wk", wait_keys)
    run("q1", send_queries, 1)
    run("p2", late_audio, 1)
    run("a0", attend_rows, 0)
    run("q2", send_queries, 2)
    run("a1", attend_rows, 1)
    run("ca", cross_audio)
    run("A0", share_rows, 0)
    run("PL", cross_part)
    @pl.when(core == 0)
    def _():
        run("B0", send_far, 0)

    run("a2", attend_rows, 2)
    @pl.when(core == 1)
    def _():
        run("B0", send_far, 0)

    @pl.when(core == 1)
    def _():
        run("PR", relay_part)

    run("A1", share_rows, 1)
    run("B1", send_far, 1)
    @pl.when(core == 0)
    def _():
        run("PR", relay_part)

    run("cs", cross_send)
    run("A2", share_parts, 2)
    @pl.when(core == 1)
    def _():
        run("k0", give_home)

    @pl.when(core == 1)
    def _():
        run("k1", keep_home)

    run("B2", send_far, 2)
    @pl.when(core == 0)
    def _():
        run("k0", give_home)

    @pl.when(core == 0)
    def _():
        run("k1", keep_home)

    run("cf", cross_finish)
    run("cv", cross_video)
    run("h", home_copy.wait_recv)
    run("c0", close_rows, 0)
    run("c1", close_rows, 1)
    run("c2", close_rows, 2)
    with jax.named_scope("settle"):
        settle()


def write_out(*refs):
    half = len(refs) // 2
    for src, dst in zip(refs[:half], refs[half:]):
        dst[...] = src[...]


def fused(seq, tensor, *operands):
    vq, vk, vv, vs, weight, cq, ak, av, aq, ck, cv = operands
    rows, features = vq.shape
    span = features // seq
    audio_rows, cross_width = aq.shape
    chips = tensor // 2
    width = weight.shape[1] // tensor
    groups = len(row_cuts(rows))
    others = max(chips - 1, 1)
    bf16, f32, dma = jnp.bfloat16, jnp.float32, pltpu.SemaphoreType.DMA
    shapes = tuple(jax.ShapeDtypeStruct(x.shape, bf16) for x in (vs, cq, aq))
    whole = pl.BlockSpec(memory_space=pltpu.VMEM)
    results = pl.pallas_call(
        functools.partial(block_kernel, seq, tensor),
        out_shape=tuple(pltpu.VMEM(x.shape, bf16) for x in (vs, cq, aq)),
        in_specs=[pl.BlockSpec(memory_space=pltpu.HBM)] * 11,
        out_specs=(whole,) * 3,
        scratch_shapes=[
            pltpu.VMEM((2, seq * rows, span), bf16),
            pltpu.VMEM((seq * rows, span), bf16),
            pltpu.VMEM((seq * rows, span), bf16),
            pltpu.VMEM((seq, rows, span), bf16),
            pltpu.VMEM((3, seq * audio_rows, cross_width), bf16),
            pltpu.VMEM((seq * audio_rows, cross_width + HD), bf16),
            pltpu.VMEM((seq, audio_rows, cross_width + HD), bf16),
            pltpu.VMEM((3, *cq.shape), bf16),
            pltpu.VMEM(vs.shape, bf16),
            pltpu.VMEM(weight.shape, bf16),
            pltpu.VMEM(vs.shape, f32),
            pltpu.VMEM((others, rows, width), f32),
            pltpu.VMEM((others, rows, width), f32),
            pltpu.VMEM((chips, rows, width), bf16),
            pltpu.VMEM((chips, rows, width), bf16),
            pltpu.VMEM((others, rows, width), bf16),
            pltpu.VMEM((others, rows, width), bf16),
            pltpu.SemaphoreType.REGULAR((2,)),
            pltpu.SemaphoreType.REGULAR((1,)),
            dma(()),
            dma(()),
            dma(()),
            dma((groups,)),
            dma(()),
            dma(()),
            dma((groups,)),
            dma((seq,)),
            dma((2,)),
            dma((2, seq)),
            dma(()),
            dma(()),
            dma(()),
            dma(()),
            dma(()),
            dma(()),
            dma(()),
            dma((groups, others)),
            dma(()),
            dma(()),
            dma((groups, others)),
        ],
        compiler_params=pltpu.CompilerParams(
            collective_id=0, has_side_effects=True, vmem_limit_bytes=60000000
        ),
    )(*operands)
    return pl.pallas_call(
        write_out,
        out_shape=shapes,
        in_specs=[whole] * 3,
        out_specs=(whole,) * 3,
        compiler_params=pltpu.CompilerParams(vmem_limit_bytes=8 * 2**20),
    )(*results)


def fits(mesh, operands):
    seq, tensor = mesh.shape["seq"], mesh.shape["tensor"]
    vq, weight, cq, aq = operands[0], operands[4], operands[5], operands[8]
    return (
        seq > 1
        and (vq.shape[1] // HD) % seq == 0
        and tensor % 2 == 0
        and (weight.shape[1] // tensor) % WIDE == 0
        and aq.shape[0] % 16 == 0
        and vq.shape[0] % 16 == 0
        and 6 * (cq.shape[1] // HD) <= HD
        and (aq.size * seq) % (vq.shape[1] * 16) == 0
        and 2 * (seq + 1) * aq.size <= vq.size
        and weight.size * 2 <= 10 * 2**20
        and vq.shape[0] <= 128
        and seq <= 8
    )


def solution(mesh):
    def step(*operands):
        if fits(mesh, operands):
            return fused(mesh.shape["seq"], mesh.shape["tensor"], *operands)
        return local(*operands)

    in_specs = (
        P(("groups", "seq"), "tensor"),
        P(("groups", "seq"), "tensor"),
        P(("groups", "seq"), "tensor"),
        P(("groups", "seq"), "tensor"),
        P("tensor", None),
        P(("groups", "seq"), "tensor"),
        P(("groups", "seq"), "tensor"),
        P(("groups", "seq"), "tensor"),
        P(("groups", "seq"), "tensor"),
        P(("groups", "seq"), "tensor"),
        P(("groups", "seq"), "tensor"),
    )
    out_specs = (
        P(("groups", "seq"), "tensor"),
        P(("groups", "seq"), "tensor"),
        P(("groups", "seq"), "tensor"),
    )
    return jax.shard_map(step, mesh=mesh, in_specs=in_specs, out_specs=out_specs, check_vma=False)
```

```python
import functools
import math

import jax
import jax.numpy as jnp
from jax import lax
from jax.experimental import pallas as pl
from jax.experimental.pallas import tpu as pltpu
from jax.sharding import PartitionSpec as P

HD = 128


def blank_state(query_rows, head_count):
    return (
        jnp.full((head_count, query_rows), -1e30, jnp.float32),
        jnp.zeros((head_count, query_rows), jnp.float32),
        jnp.zeros((head_count, query_rows, HD), jnp.float32),
    )


def absorb(carried, queries, keyset, values, head_count):
    running, row_sum, numerator = carried
    query_rows = queries.shape[0]
    key_rows = keyset.shape[0]
    factor = 1.0 / math.sqrt(HD)
    query_heads = queries.reshape(query_rows, head_count, HD)
    for offset in range(0, key_rows, 1024):
        width_keys = min(1024, key_rows - offset)
        key_block = keyset[offset : offset + width_keys].reshape(width_keys, head_count, HD)
        value_block = values[offset : offset + width_keys].reshape(width_keys, head_count, HD)
        scores = (
            jnp.einsum("qhd,khd->hqk", query_heads, key_block, preferred_element_type=jnp.float32)
            * factor
        )
        highest = jnp.maximum(running, jnp.max(scores, axis=2))
        raised = jnp.exp(scores - highest[:, :, None])
        shrink = jnp.exp(running - highest)
        row_sum = row_sum * shrink + jnp.sum(raised, axis=2)
        numerator = numerator * shrink[:, :, None] + jnp.einsum(
            "hqk,khd->hqd",
            raised.astype(jnp.bfloat16),
            value_block,
            preferred_element_type=jnp.float32,
        )
        running = highest
    return (running, row_sum, numerator)


def finish(carried, head_count):
    running, row_sum, numerator = carried
    result = numerator / row_sum[:, :, None]
    return result.transpose(1, 0, 2).reshape(result.shape[1], head_count * HD).astype(jnp.bfloat16)


def local(
    video_query,
    video_key,
    video_value,
    video_stream,
    out_weight,
    cross_query,
    audio_key,
    audio_value,
    audio_query,
    cross_key,
    cross_value,
):
    local_heads = video_query.shape[1] // HD
    query_rows = video_query.shape[0]
    pieces = (
        lax.all_gather(video_key, "seq", axis=0, tiled=True),
        lax.all_gather(video_value, "seq", axis=0, tiled=True),
    )
    carried_video = absorb(
        blank_state(query_rows, local_heads), video_query, pieces[0], pieces[1], local_heads
    )
    attended = finish(carried_video, local_heads)
    projected = jnp.dot(attended, out_weight, preferred_element_type=jnp.float32)
    summed = lax.psum_scatter(
        projected.astype(jnp.bfloat16), "tensor", scatter_dimension=1, tiled=True
    ).astype(jnp.float32)
    video_next = (video_stream.astype(jnp.float32) + summed).astype(jnp.bfloat16)
    cross_heads = cross_query.shape[1] // HD
    every_key, every_value = (
        lax.all_gather(audio_key, "seq", axis=0, tiled=True),
        lax.all_gather(audio_value, "seq", axis=0, tiled=True),
    )
    carried_audio = absorb(
        blank_state(cross_query.shape[0], cross_heads),
        cross_query,
        every_key,
        every_value,
        cross_heads,
    )
    video_cross = finish(carried_audio, cross_heads)
    pieces = (
        lax.all_gather(cross_key, "seq", axis=0, tiled=True),
        lax.all_gather(cross_value, "seq", axis=0, tiled=True),
    )
    carried_cross = absorb(
        blank_state(audio_query.shape[0], cross_heads),
        audio_query,
        pieces[0],
        pieces[1],
        cross_heads,
    )
    audio_cross = finish(carried_cross, cross_heads)
    return (video_next, video_cross, audio_cross)


MESH = pl.DeviceIdType.MESH
NT = (((1,), (1,)), ((), ()))
WIDE = 512
SHARES = (4, 3, 1)
SPLIT = True


def softmax_parts(queries, keyset, values):
    scores = lax.dot_general(queries, keyset, NT, preferred_element_type=jnp.float32) * (
        1.0 / math.sqrt(HD)
    )
    highest = jnp.max(scores, axis=1, keepdims=True)
    raised = jnp.exp(scores - highest)
    row_sum = jnp.sum(raised, axis=1, keepdims=True)
    numerator = jnp.dot(raised.astype(jnp.bfloat16), values, preferred_element_type=jnp.float32)
    return highest, row_sum, numerator


def row_cuts(rows):
    tiles, whole = rows // 16, sum(SHARES)
    marks = sorted({tiles * sum(SHARES[: i + 1]) // whole for i in range(len(SHARES))} | {0})
    return [(16 * a, 16 * (b - a)) for a, b in zip(marks, marks[1:])]


def by_distance(me, seq):
    right = (me < seq - 1 - me).astype(jnp.int32)
    toward = 2 * right - 1
    short = right * me + (1 - right) * (seq - 1 - me)
    order = []
    for i in range(seq - 1):
        both = (i < 2 * short).astype(jnp.int32)
        near = (i // 2 + 1) * (1 if i % 2 == 0 else -1)
        order.append(me + toward * (both * near + (1 - both) * (i - short + 1)))
    return order


def block_kernel(
    seq,
    tensor,
    vq,
    vk,
    vv,
    vs,
    weight,
    cq,
    ak,
    av,
    aq,
    ck,
    cv,
    next_ref,
    vcross_ref,
    across_ref,
    kv,
    q_all,
    heads_out,
    gathered,
    audio,
    partial,
    partial_in,
    cross_v,
    stream_v,
    weight_v,
    kept,
    mine,
    other,
    pair_out,
    pair_in,
    far_out,
    far_in,
    token,
    beside,
    kv_send,
    kv_recv,
    q_send,
    q_recv,
    own_sem,
    out_send,
    out_recv,
    out_last,
    audio_send,
    audio_recv,
    audio_own,
    part_send,
    part_recv,
    cross_sem,
    stream_sem,
    weight_sem,
    pair_send,
    pair_recv,
    home_recv,
    far_send,
    far_recv,
):
    rows = vq.shape[0]
    span = vq.shape[1] // seq
    share = span // HD
    cross_heads = cq.shape[1] // HD
    audio_rows, cross_width = aq.shape
    chips = tensor // 2
    width = next_ref.shape[1]
    pieces = width // WIDE
    cuts = row_cuts(rows)
    groups = len(cuts)
    me = lax.axis_index("seq")
    place = lax.axis_index("tensor")
    core = lax.rem(place, 2)
    chip = place // 2
    sibling = chip * 2 + (1 - core)
    peers = by_distance(me, seq)
    far_chips = [lax.rem(chip + d, chips) for d in range(chips)]

    def rows_of(p):
        return pl.ds(pl.multiple_of(p * rows, rows), rows)

    def audio_rows_of(p):
        return pl.ds(pl.multiple_of(p * audio_rows, audio_rows), audio_rows)

    def cols_of(p):
        return pl.ds(pl.multiple_of(p * span, span), span)

    def slot(p, r):
        start, size = cuts[r]
        return pl.ds(pl.multiple_of(seq * start + p * size, 16), size)

    for kind, ref in enumerate((vk, vv)):
        pltpu.make_async_copy(ref.at[:, cols_of(me)], kv.at[kind, rows_of(me)], own_sem).start()
    for r in range(groups):
        pltpu.make_async_copy(vq.at[pl.ds(*cuts[r]), cols_of(me)], q_all.at[slot(me, r)], own_sem).start()
    for kind, ref in enumerate((ak, av, aq)):
        pltpu.make_async_copy(ref, audio.at[kind, audio_rows_of(me)], audio_own).start()
    for kind, ref in enumerate((cq, ck, cv)):
        pltpu.make_async_copy(ref, cross_v.at[kind], cross_sem).start()
    stream_copy = pltpu.make_async_copy(vs, stream_v, stream_sem)
    stream_copy.start()

    def local_done(ref, sem):
        pltpu.make_async_copy(ref, ref, sem).wait()

    barrier = pltpu.get_barrier_semaphore()
    for way in (1, -1):

        @pl.when((me + way >= 0) & (me + way < seq))
        def _():
            pl.semaphore_signal(barrier, inc=1, device_id={"seq": me + way}, device_id_type=MESH)

    pl.semaphore_signal(barrier, inc=1, device_id={"tensor": sibling}, device_id_type=MESH)
    for d in range(1, chips):
        pl.semaphore_signal(
            barrier, inc=1, device_id={"tensor": far_chips[d] * 2 + core}, device_id_type=MESH
        )
    inner = ((me > 0) & (me < seq - 1)).astype(jnp.int32)
    with jax.named_scope("barrier"):
        pl.semaphore_wait(barrier, chips + 1 + inner)

    def to_seq(src, dst, send_sem, recv_sem, p):
        return pltpu.make_async_remote_copy(
            src_ref=src,
            dst_ref=dst,
            send_sem=send_sem,
            recv_sem=recv_sem,
            device_id={"seq": p},
            device_id_type=MESH,
        )

    def all_of(ref, send_sem, recv_sem):
        return to_seq(ref, ref, send_sem, recv_sem, peers[0])

    def keys_to(p, kinds=(0, 1)):
        for kind, ref in zip(kinds, (vk, vv)[kinds[0] :]):
            to_seq(ref.at[:, cols_of(p)], kv.at[kind, rows_of(me)], kv_send, kv_recv, p).start()

    def send_queries(r):
        here = pl.ds(*cuts[r])
        for p in peers[::-1]:
            to_seq(vq.at[here, cols_of(p)], q_all.at[slot(me, r)], q_send, q_recv.at[r], p).start()

    def audio_hop(step, way, part):
        shard = lax.rem(me - way * step + seq, seq)
        here = audio_rows_of(shard)
        block = audio.at[2, here] if part else audio.at[pl.ds(0, 2), here]
        return to_seq(
            block,
            block,
            audio_send.at[part],
            audio_recv.at[part, shard],
            lax.rem(me + way + seq, seq),
        )

    def on_line(step, way):
        source, target = me - way * step, me + way
        return (source >= 0) & (source < seq) & (target >= 0) & (target < seq)

    def pass_audio(step, part):
        for way in (1, -1):

            @pl.when(on_line(step, way))
            def _():
                copy = audio_hop(step, way, part)
                if step:
                    copy.wait_recv()
                copy.start()

    def crosses(way):
        return me == (seq // 2 - 1 if way > 0 else seq // 2)

    def some_audio(steps, chosen):
        for step in steps:
            for way in (1, -1):

                @pl.when(on_line(step, way) & chosen(step, way))
                def _():
                    copy = audio_hop(step, way, 0)
                    if step:
                        copy.wait_recv()
                    copy.start()

    def early_part():
        some_audio((0,), lambda step, way: jnp.logical_not(crosses(way)))

    def cross_part():
        some_audio((0, 1), lambda step, way: crosses(way))

    def relay_part():
        some_audio(range(1, seq - 1), lambda step, way: (step > 1) | jnp.logical_not(crosses(way)))

    def end_audio(part):
        for step in range(1, seq):
            for way in (1, -1):
                source, target = me - way * step, me + way
                last = (target < 0) | (target >= seq)

                @pl.when((source >= 0) & (source < seq) & last)
                def _():
                    audio_hop(step, way, part).wait_recv()

    def token_to(way):
        pl.semaphore_signal(
            token.at[(way + 1) // 2], inc=1, device_id={"seq": me + way}, device_id_type=MESH
        )

    def within(p):
        return (p >= 0) & (p < seq)

    def first_tokens():
        for way in (1, -1):

            @pl.when(within(me - way) & jnp.logical_not(within(me - 2 * way)) & within(me + way))
            def _():
                token_to(way)

    def tokens():
        for way in (1, -1):

            @pl.when(within(me - 2 * way))
            def _():
                pl.semaphore_wait(token.at[(way + 1) // 2], 1)

            @pl.when(within(me - 2 * way) & within(me + way))
            def _():
                token_to(way)

    local_done(audio.at[:, audio_rows_of(0)], audio_own)
    def run(name, f, *args):
        with jax.named_scope(name):
            f(*args)

    def late_audio(part):
        for step in range(2, seq - 1):
            pass_audio(step, part)

    def meet():
        pl.semaphore_signal(
            beside.at[0], inc=1, device_id={"tensor": sibling}, device_id_type=MESH
        )
        pl.semaphore_wait(beside.at[0], 1)

    run("p0", pass_audio, 0, 1)
    run("K0", keys_to, peers[0])
    run("tk1", first_tokens)
    run("tok", tokens)
    run("sib", meet)
    run("K2", keys_to, peers[2])
    run("K1", keys_to, peers[1])
    run("q0", send_queries, 0)
    run("PE", early_part)
    run("p1", pass_audio, 1, 1)
    weight_copy = pltpu.make_async_copy(weight, weight_v, weight_sem)
    weight_copy.start()

    def wait_keys():
        local_done(kv.at[:, pl.ds(0, rows * 3 // 2)], own_sem)
        all_of(kv.at[:, pl.ds(0, (seq - 1) * rows)], kv_send, kv_recv).wait_recv()

    def attend_rows(r):
        start, size = cuts[r]
        all_of(q_all.at[pl.ds(0, (seq - 1) * size)], q_send, q_recv.at[r]).wait_recv()
        block = pl.ds(seq * start, seq * size)
        for h in range(share):
            cols = slice(h * HD, (h + 1) * HD)
            _, row_sum, numerator = softmax_parts(q_all[block, cols], kv[0, :, cols], kv[1, :, cols])
            heads_out[block, cols] = (numerator / row_sum).astype(jnp.bfloat16)
        here = pl.ds(start, size)
        for p in peers[::-1]:
            sem = out_last.at[me] if SPLIT and r == groups - 1 else out_recv.at[r]
            to_seq(heads_out.at[slot(p, r)], gathered.at[me, here], out_send, sem, p).start()
        gathered[me, here] = heads_out[slot(me, r)]

    def upper(value):
        return value.astype(jnp.bfloat16).astype(jnp.float32)

    def cross_audio():
        local_done(cross_v, cross_sem)
        end_audio(1)
        lane = lax.broadcasted_iota(jnp.int32, (seq * audio_rows, HD), 1)
        held = jnp.zeros((seq * audio_rows, HD), jnp.float32)
        for c in range(cross_heads):
            cols = slice(c * HD, (c + 1) * HD)
            highest, row_sum, numerator = softmax_parts(
                audio[2, :, cols], cross_v[1, :, cols], cross_v[2, :, cols]
            )
            for i, value in enumerate((highest, row_sum)):
                for k in range(3):
                    piece = upper(value)
                    held = jnp.where(lane == 3 * (2 * c + i) + k, piece, held)
                    value = value - piece
            partial[:, cols] = numerator.astype(jnp.bfloat16)
        partial[:, cross_heads * HD :] = held.astype(jnp.bfloat16)

    def cross_video():
        end_audio(0)
        for c in range(cross_heads):
            cols = slice(c * HD, (c + 1) * HD)
            _, row_sum, numerator = softmax_parts(
                cross_v[0, :, cols], audio[0, :, cols], audio[1, :, cols]
            )
            vcross_ref[:, cols] = (numerator / row_sum).astype(jnp.bfloat16)

    def cross_send():
        for p in peers:
            theirs = audio_rows_of(p)
            to_seq(partial.at[theirs], partial_in.at[me], part_send, part_recv, p).start()

    def cross_finish():
        all_of(partial_in.at[pl.ds(0, seq - 1)], part_send, part_recv).wait_recv()
        my_audio = audio_rows_of(me)
        stat_cols = slice(cross_heads * HD, (cross_heads + 1) * HD)
        held = [partial[my_audio, stat_cols]] + [partial_in[p, :, stat_cols] for p in peers]
        held = [value.astype(jnp.float32) for value in held]

        def stat(s, i):
            return s[:, 3 * i : 3 * i + 1] + s[:, 3 * i + 1 : 3 * i + 2] + s[:, 3 * i + 2 : 3 * i + 3]

        for c in range(cross_heads):
            cols = slice(c * HD, (c + 1) * HD)
            parts = [partial[my_audio, cols]] + [partial_in[p, :, cols] for p in peers]
            tops = [stat(s, 2 * c) for s in held]
            sums = [stat(s, 2 * c + 1) for s in held]
            highest = functools.reduce(jnp.maximum, tops)
            factors = [jnp.exp(t - highest) for t in tops]
            row_sum = sum(f * s for f, s in zip(factors, sums))
            numerator = sum(f * n.astype(jnp.float32) for f, n in zip(factors, parts))
            across_ref[:, cols] = (numerator / row_sum).astype(jnp.bfloat16)

    def product(attended, d, side, j):
        target = far_chips[d] * 2 + (core if side else 1 - core)
        cols = pl.ds(pl.multiple_of(target * width + j * WIDE, WIDE), WIDE)
        return jnp.dot(attended, weight_v[:, cols], preferred_element_type=jnp.float32)

    def pair_copy(r, d):
        here = pl.ds(*cuts[r])
        return pltpu.make_async_remote_copy(
            src_ref=pair_out.at[d, here],
            dst_ref=pair_in.at[d, here],
            send_sem=pair_send,
            recv_sem=pair_recv.at[r, d - 1],
            device_id={"tensor": sibling},
            device_id_type=MESH,
        )

    def far_copy(r, d):
        here = pl.ds(*cuts[r])
        return pltpu.make_async_remote_copy(
            src_ref=far_out.at[d - 1, here],
            dst_ref=far_in.at[d - 1, here],
            send_sem=far_send,
            recv_sem=far_recv.at[r, d - 1],
            device_id={"tensor": far_chips[d] * 2 + core},
            device_id_type=MESH,
        )

    home_copy = pltpu.make_async_remote_copy(
        src_ref=pair_out.at[0],
        dst_ref=pair_in.at[0],
        send_sem=pair_send,
        recv_sem=home_recv,
        device_id={"tensor": sibling},
        device_id_type=MESH,
    )
    blocks = [slice(j * WIDE, (j + 1) * WIDE) for j in range(pieces)]

    def share_rows(r):
        here = pl.ds(*cuts[r])
        all_of(gathered.at[pl.ds(0, seq - 1), here], out_send, out_recv.at[r]).wait_recv()
        attended = jnp.concatenate([gathered[p, here] for p in range(seq)], axis=1)
        if r == 0:
            weight_copy.wait()
        for d in range(1, chips):
            for j, block in enumerate(blocks):
                pair_out[d, here, block] = product(attended, d, 0, j).astype(jnp.bfloat16)
            pair_copy(r, d).start()
        for d in range(1, chips):
            for j, block in enumerate(blocks):
                mine[d - 1, here, block] = product(attended, d, 1, j)

    def share_parts(r):
        here = pl.ds(*cuts[r])

        def add_part(some, d, side, first):
            target = far_chips[d] * 2 + (core if side else 1 - core)
            for j, block in enumerate(blocks):
                cols = pl.ds(pl.multiple_of(target * width + j * WIDE, WIDE), WIDE)
                value = sum(
                    jnp.dot(gathered[p, here], weight_v[cols_of(p), cols], preferred_element_type=jnp.float32)
                    for p in some
                )
                ref = mine if side else other
                ref[d - 1, here, block] = value if first else ref[d - 1, here, block] + value

        some = [me]
        for i, p in enumerate(peers):
            all_of(gathered.at[0, here], out_send, out_last.at[p]).wait_recv()
            some.append(p)
            if i == 0 and len(peers) > 1:
                continue
            for side in (0, 1):
                for d in range(1, chips):
                    add_part(some, d, side, i <= 1)
                    if side == 0 and i == len(peers) - 1:
                        pair_out[d, here] = other[d - 1, here].astype(jnp.bfloat16)
                        pair_copy(r, d).start()
            some = []

    def send_far(r):
        here = pl.ds(*cuts[r])
        for d in range(1, chips):
            pair_copy(r, d).wait_recv()
            far_out[d - 1, here] = (mine[d - 1, here] + pair_in[d, here].astype(jnp.float32)).astype(
                jnp.bfloat16
            )
            far_copy(r, d).start()

    def all_heads():
        return jnp.concatenate([gathered[p] for p in range(seq)], axis=1)

    def give_home():
        attended = all_heads()
        for j, block in enumerate(blocks):
            pair_out[0, :, block] = product(attended, 0, 0, j).astype(jnp.bfloat16)
        home_copy.start()

    def keep_home():
        attended = all_heads()
        stream_copy.wait()
        for j, block in enumerate(blocks):
            kept[:, block] = product(attended, 0, 1, j) + stream_v[:, block].astype(jnp.float32)

    def close_rows(r):
        here = pl.ds(*cuts[r])
        value = kept[here] + pair_in[0, here].astype(jnp.float32)
        for d in range(1, chips):
            far_copy(r, d).wait_recv()
            value = value + far_in[d - 1, here].astype(jnp.float32)
        next_ref[here] = value.astype(jnp.bfloat16)

    def settle():
        all_of(kv.at[:, pl.ds(0, (seq - 1) * rows)], kv_send, kv_recv).wait_send()
        all_of(q_all.at[pl.ds(0, (seq - 1) * rows)], q_send, q_recv.at[0]).wait_send()
        all_of(heads_out.at[pl.ds(0, (seq - 1) * rows)], out_send, out_recv.at[0]).wait_send()
        all_of(partial.at[pl.ds(0, (seq - 1) * audio_rows)], part_send, part_recv).wait_send()
        block = audio_rows * cross_width // span
        for part, count in ((0, 2), (1, 1)):
            for hops, place_fits in ((1, inner == 0), (seq + 1, inner == 1)):

                @pl.when(place_fits)
                def _():
                    some = heads_out.at[pl.ds(0, hops * count * block)]
                    all_of(some, audio_send.at[part], audio_recv.at[part, 0]).wait_send()

        all_of(pair_out, pair_send, pair_recv.at[0, 0]).wait_send()
        if chips > 1:
            all_of(far_out, far_send, far_recv.at[0, 0]).wait_send()

    run("wk", wait_keys)
    run("q1", send_queries, 1)
    run("p2", late_audio, 1)
    run("a0", attend_rows, 0)
    run("q2", send_queries, 2)
    run("a1", attend_rows, 1)
    run("ca", cross_audio)
    run("A0", share_rows, 0)
    run("PL", cross_part)
    @pl.when(core == 0)
    def _():
        run("B0", send_far, 0)

    run("a2", attend_rows, 2)
    @pl.when(core == 1)
    def _():
        run("B0", send_far, 0)

    @pl.when(core == 1)
    def _():
        run("PR", relay_part)

    run("A1", share_rows, 1)
    run("B1", send_far, 1)
    @pl.when(core == 0)
    def _():
        run("PR", relay_part)

    run("cs", cross_send)
    run("A2", share_parts, 2)
    @pl.when(core == 1)
    def _():
        run("k0", give_home)

    @pl.when(core == 1)
    def _():
        run("k1", keep_home)

    run("B2", send_far, 2)
    @pl.when(core == 0)
    def _():
        run("k0", give_home)

    @pl.when(core == 0)
    def _():
        run("k1", keep_home)

    run("cf", cross_finish)
    run("cv", cross_video)
    run("h", home_copy.wait_recv)
    run("c0", close_rows, 0)
    run("c1", close_rows, 1)
    run("c2", close_rows, 2)
    with jax.named_scope("settle"):
        settle()


def write_out(*refs):
    half = len(refs) // 2
    for src, dst in zip(refs[:half], refs[half:]):
        dst[...] = src[...]


def fused(seq, tensor, *operands):
    vq, vk, vv, vs, weight, cq, ak, av, aq, ck, cv = operands
    rows, features = vq.shape
    span = features // seq
    audio_rows, cross_width = aq.shape
    chips = tensor // 2
    width = weight.shape[1] // tensor
    groups = len(row_cuts(rows))
    others = max(chips - 1, 1)
    bf16, f32, dma = jnp.bfloat16, jnp.float32, pltpu.SemaphoreType.DMA
    shapes = tuple(jax.ShapeDtypeStruct(x.shape, bf16) for x in (vs, cq, aq))
    whole = pl.BlockSpec(memory_space=pltpu.VMEM)
    results = pl.pallas_call(
        functools.partial(block_kernel, seq, tensor),
        out_shape=tuple(pltpu.VMEM(x.shape, bf16) for x in (vs, cq, aq)),
        in_specs=[pl.BlockSpec(memory_space=pltpu.HBM)] * 11,
        out_specs=(whole,) * 3,
        scratch_shapes=[
            pltpu.VMEM((2, seq * rows, span), bf16),
            pltpu.VMEM((seq * rows, span), bf16),
            pltpu.VMEM((seq * rows, span), bf16),
            pltpu.VMEM((seq, rows, span), bf16),
            pltpu.VMEM((3, seq * audio_rows, cross_width), bf16),
            pltpu.VMEM((seq * audio_rows, cross_width + HD), bf16),
            pltpu.VMEM((seq, audio_rows, cross_width + HD), bf16),
            pltpu.VMEM((3, *cq.shape), bf16),
            pltpu.VMEM(vs.shape, bf16),
            pltpu.VMEM(weight.shape, bf16),
            pltpu.VMEM(vs.shape, f32),
            pltpu.VMEM((others, rows, width), f32),
            pltpu.VMEM((others, rows, width), f32),
            pltpu.VMEM((chips, rows, width), bf16),
            pltpu.VMEM((chips, rows, width), bf16),
            pltpu.VMEM((others, rows, width), bf16),
            pltpu.VMEM((others, rows, width), bf16),
            pltpu.SemaphoreType.REGULAR((2,)),
            pltpu.SemaphoreType.REGULAR((1,)),
            dma(()),
            dma(()),
            dma(()),
            dma((groups,)),
            dma(()),
            dma(()),
            dma((groups,)),
            dma((seq,)),
            dma((2,)),
            dma((2, seq)),
            dma(()),
            dma(()),
            dma(()),
            dma(()),
            dma(()),
            dma(()),
            dma(()),
            dma((groups, others)),
            dma(()),
            dma(()),
            dma((groups, others)),
        ],
        compiler_params=pltpu.CompilerParams(
            collective_id=0, has_side_effects=True, vmem_limit_bytes=60000000
        ),
    )(*operands)
    return pl.pallas_call(
        write_out,
        out_shape=shapes,
        in_specs=[whole] * 3,
        out_specs=(whole,) * 3,
        compiler_params=pltpu.CompilerParams(vmem_limit_bytes=8 * 2**20),
    )(*results)


def fits(mesh, operands):
    seq, tensor = mesh.shape["seq"], mesh.shape["tensor"]
    vq, weight, cq, aq = operands[0], operands[4], operands[5], operands[8]
    return (
        seq > 1
        and (vq.shape[1] // HD) % seq == 0
        and tensor % 2 == 0
        and (weight.shape[1] // tensor) % WIDE == 0
        and aq.shape[0] % 16 == 0
        and vq.shape[0] % 16 == 0
        and 6 * (cq.shape[1] // HD) <= HD
        and (aq.size * seq) % (vq.shape[1] * 16) == 0
        and 2 * (seq + 1) * aq.size <= vq.size
        and weight.size * 2 <= 10 * 2**20
        and vq.shape[0] <= 128
        and seq <= 8
    )


def solution(mesh):
    def step(*operands):
        if fits(mesh, operands):
            return fused(mesh.shape["seq"], mesh.shape["tensor"], *operands)
        return local(*operands)

    in_specs = (
        P(("groups", "seq"), "tensor"),
        P(("groups", "seq"), "tensor"),
        P(("groups", "seq"), "tensor"),
        P(("groups", "seq"), "tensor"),
        P("tensor", None),
        P(("groups", "seq"), "tensor"),
        P(("groups", "seq"), "tensor"),
        P(("groups", "seq"), "tensor"),
        P(("groups", "seq"), "tensor"),
        P(("groups", "seq"), "tensor"),
        P(("groups", "seq"), "tensor"),
    )
    out_specs = (
        P(("groups", "seq"), "tensor"),
        P(("groups", "seq"), "tensor"),
        P(("groups", "seq"), "tensor"),
    )
    return jax.shard_map(step, mesh=mesh, in_specs=in_specs, out_specs=out_specs, check_vma=False)
```
